32 devices in a mesh: row: 4 (over z), col: 8 (over y, x, core).
Axes of the slice: x: 2, y: 2, z: 4, core: 2. Of those that a mesh axis runs over, the one named last changes fastest.
Arguments:
- pair: bfloat16 [256, 256, 128], P('row', 'col'), may hold values from -6 to 6
- residue_mask: int32 [256], replicated, may hold values 0 or 1
- norm_gain: float32 [2, 2, 128], replicated, may hold values from 0.25 to 1.75
- norm_bias: float32 [2, 2, 128], replicated, may hold values from -3 to 3
- w_in_q: bfloat16 [2, 128, 640], replicated, may hold values from -0.5 to 0.5
- exp_in: int32 [2, 4, 20], replicated, may hold values from -2 to 1
- w_out_q: bfloat16 [2, 128, 128], replicated, may hold values from -0.5 to 0.5
- exp_out: int32 [2, 4, 4], replicated, may hold values from -2 to 1
Outputs:
- pair_out: bfloat16 [256, 256, 128], P('row', 'col')
The draws below stay inside these ranges and needn't reach their ends.
All inputs are finite; a program needn't handle non-finite values.
Results may differ from the reference program's by a relative error of at most 0.0056.
Values may be sent and summed in bfloat16 or wider, within the bound.
No kernel may reach another device: no remote copies, remote signals or barrier semaphores. Data moves between devices by JAX's collectives and lax.ppermute only.
A program may use at most 128 MiB of HBM per device.

```python
import jax
import jax.numpy as jnp
from jax import lax

C = 128
BLK = 32
N = 256


def set_ends(array, stream_key, low, high):
    dims = array.shape
    spot = [jax.random.randint(jax.random.fold_in(stream_key, axis), (), 0, dims[axis]) for axis in range(len(dims))]
    array = array.at[tuple(spot)].set(low)
    longest = dims.index(max(dims))
    spot[longest] = (spot[longest] + 1) % dims[longest]
    return array.at[tuple(spot)].set(high)


def shard_levels(key, shape, shards, least, top_value):
    factor_of, own = 1.0, jax.random.fold_in(key, 6)
    for dim, parts in shards:
        draws = jnp.exp(jax.random.uniform(jax.random.fold_in(own, dim), (parts,), jnp.float32, least / len(shards), top_value / len(shards)))
        factor_of = factor_of * jnp.repeat(draws, shape[dim] // parts).reshape([-1 if axis == dim else 1 for axis in range(len(shape))])
    return factor_of


def noise(own_key, extent, scale, limit, cuts=(), dtype=jnp.bfloat16):
    array = jax.random.normal(own_key, extent, jnp.float32) * scale
    if len(cuts) > 0:
        array = shard_levels(own_key, extent, cuts, -0.22, 0.18) * array
    return jnp.clip(array, min=-limit, max=limit).astype(dtype)


def setup_inputs(seed: int = 0) -> dict:
    arg_keys = jax.random.split(jax.random.key(seed), 9)
    pair = noise(arg_keys[0], (N, N, C), 1.0, 6.0, ((0, 4), (1, 8)))
    residue_mask = set_ends((jax.random.randint(arg_keys[1], (N,), 0, 8) < 7).astype(jnp.int32), jax.random.fold_in(arg_keys[1], 1), 0, 1)
    norm_gain = jnp.clip(1.0 + 0.15 * jax.random.normal(arg_keys[2], (2, 2, C), jnp.float32), 0.25, 1.75)
    norm_bias = noise(arg_keys[3], (2, 2, C), 0.5, 3.0, (), jnp.float32)
    w_in_q = noise(arg_keys[4], (2, C, 5 * C), C ** -0.5, 0.5)
    exp_in = set_ends(jax.random.randint(arg_keys[5], (2, C // BLK, 5 * C // BLK), -2, 2), jax.random.fold_in(arg_keys[5], 1), -2, 1).astype(jnp.int32)
    w_out_q = noise(arg_keys[6], (2, C, C), C ** -0.5, 0.5)
    exp_out = set_ends(jax.random.randint(arg_keys[7], (2, C // BLK, C // BLK), -2, 2), jax.random.fold_in(arg_keys[7], 1), -2, 1).astype(jnp.int32)
    return {"pair": pair, "residue_mask": residue_mask, "norm_gain": norm_gain, "norm_bias": norm_bias, "w_in_q": w_in_q, "exp_in": exp_in, "w_out_q": w_out_q, "exp_out": exp_out}


def layer_norm(values, scale_vec, shift_vec):
    average = lax.optimization_barrier(jnp.mean(values, axis=-1, keepdims=True))
    centred = values - average
    variance = lax.optimization_barrier(jnp.mean(centred * centred, axis=-1, keepdims=True))
    return centred * lax.rsqrt(variance + 1e-05) * scale_vec + shift_vec

def dequantize(quantized, exponents, block_size):
    scales = jnp.exp2(exponents.astype(jnp.float32))
    scales = jnp.repeat(jnp.repeat(scales, block_size, axis=0), block_size, axis=1)
    return (quantized.astype(jnp.float32) * scales).astype(jnp.bfloat16)

def project(pair_in, row_mask, col_mask, layer, norm_gain, norm_bias, w_in_q, exp_in):
    rows_n, cols_n, width = pair_in.shape
    normed = layer_norm(pair_in.astype(jnp.float32), norm_gain[layer, 0], norm_bias[layer, 0]).astype(jnp.bfloat16)
    weights_in = dequantize(w_in_q[layer], exp_in[layer], BLK)
    projected = jnp.dot(normed.reshape(rows_n * cols_n, width), weights_in, preferred_element_type=jnp.float32)
    projected = projected.reshape(rows_n, cols_n, 5 * width)
    pair_mask = (row_mask[:, None] * col_mask[None, :])[:, :, None]
    left = (jax.nn.sigmoid(projected[:, :, 0:width]) * projected[:, :, width:2 * width] * pair_mask).astype(jnp.bfloat16)
    right = (jax.nn.sigmoid(projected[:, :, 2 * width:3 * width]) * projected[:, :, 3 * width:4 * width] * pair_mask).astype(jnp.bfloat16)
    gate = jax.nn.sigmoid(projected[:, :, 4 * width:])
    return (left, right, gate)

def finish(pair_in, summed, gate, layer, norm_gain, norm_bias, w_out_q, exp_out):
    rows_n, cols_n, width = pair_in.shape
    normed = layer_norm(summed, norm_gain[layer, 1], norm_bias[layer, 1]).astype(jnp.bfloat16)
    weights_out = dequantize(w_out_q[layer], exp_out[layer], BLK)
    update = jnp.dot(normed.reshape(rows_n * cols_n, width), weights_out, preferred_element_type=jnp.float32)
    update = update.reshape(rows_n, cols_n, width)
    return (pair_in.astype(jnp.float32) + gate * update).astype(jnp.bfloat16)

def reference(pair, residue_mask, norm_gain, norm_bias, w_in_q, exp_in, w_out_q, exp_out):
    mask_all = residue_mask.astype(jnp.float32)
    left, right, gate = project(pair, mask_all, mask_all, 0, norm_gain, norm_bias, w_in_q, exp_in)
    summed = jnp.einsum('ikc,jkc->ijc', left.astype(jnp.float32), right.astype(jnp.float32))
    pair_mid = finish(pair, summed, gate, 0, norm_gain, norm_bias, w_out_q, exp_out)
    left, right, gate = project(pair_mid, mask_all, mask_all, 1, norm_gain, norm_bias, w_in_q, exp_in)
    summed = jnp.einsum('kic,kjc->ijc', left.astype(jnp.float32), right.astype(jnp.float32))
    return finish(pair_mid, summed, gate, 1, norm_gain, norm_bias, w_out_q, exp_out)
```

```python
import functools

import jax
import jax.numpy as jnp
from jax import lax
from jax.experimental import pallas as pl
from jax.experimental.pallas import tpu as pltpu
from jax.sharding import PartitionSpec as P

BLK = 32
AXES = ("row", "col")
EPS = 1e-05


def layer_norm(values, scale_vec, shift_vec):
    average = jnp.mean(values, axis=-1, keepdims=True)
    centred = values - average
    variance = jnp.mean(centred * centred, axis=-1, keepdims=True)
    return centred * lax.rsqrt(variance + EPS) * scale_vec + shift_vec


def dequantize(quantized, exponents, block_size):
    scales = jnp.exp2(exponents.astype(jnp.float32))
    scales = jnp.repeat(jnp.repeat(scales, block_size, axis=0), block_size, axis=1)
    return (quantized.astype(jnp.float32) * scales).astype(jnp.bfloat16)


def plain_update(layer, pair, row_mask, col_mask, norm_gain, norm_bias, w_in, w_out):
    rows_n, cols_n, width = pair.shape
    row_count, col_count = lax.axis_size("row"), lax.axis_size("col")
    parts = row_count * col_count
    own = width // parts
    normed = layer_norm(
        pair.astype(jnp.float32), norm_gain[layer, 0], norm_bias[layer, 0]
    ).astype(jnp.bfloat16)
    proj = jnp.einsum("ijc,cd->ijd", normed, w_in, preferred_element_type=jnp.float32)
    p0, p1, p2, p3, p4 = jnp.split(proj, 5, axis=-1)
    pm = (row_mask[:, None] * col_mask[None, :])[:, :, None]
    left = (jax.nn.sigmoid(p0) * p1 * pm).astype(jnp.bfloat16)
    right = (jax.nn.sigmoid(p2) * p3 * pm).astype(jnp.bfloat16)
    sent = jnp.stack([left, right]).reshape(2, rows_n, cols_n, parts, own)
    got = lax.all_to_all(sent.transpose(3, 0, 4, 1, 2), AXES, 0, 0, tiled=True)
    got = got.reshape(row_count, col_count, 2, own, rows_n, cols_n)
    whole = got.transpose(2, 3, 0, 4, 1, 5).reshape(
        2, own, row_count * rows_n, col_count * cols_n
    )
    spec = "cik,cjk->cij" if layer == 0 else "cki,ckj->cij"
    x = jnp.einsum(spec, whole[0], whole[1], preferred_element_type=jnp.float32)
    x = x.astype(jnp.bfloat16).reshape(own, row_count, rows_n, col_count, cols_n)
    back = x.transpose(1, 3, 0, 2, 4).reshape(parts, own, rows_n, cols_n)
    back = lax.all_to_all(back, AXES, 0, 0, tiled=True)
    x = back.transpose(2, 3, 0, 1).reshape(rows_n, cols_n, width)
    y = layer_norm(
        x.astype(jnp.float32), norm_gain[layer, 1], norm_bias[layer, 1]
    ).astype(jnp.bfloat16)
    out = jnp.einsum("ijc,cd->ijd", y, w_out, preferred_element_type=jnp.float32)
    return (pair.astype(jnp.float32) + jax.nn.sigmoid(p4) * out).astype(jnp.bfloat16)


def plain(pair, residue_mask, norm_gain, norm_bias, w_in_q, exp_in, w_out_q, exp_out):
    rows_n, cols_n, _ = pair.shape
    mask = residue_mask.astype(jnp.float32)
    row_mask = lax.dynamic_slice_in_dim(mask, lax.axis_index("row") * rows_n, rows_n)
    col_mask = lax.dynamic_slice_in_dim(mask, lax.axis_index("col") * cols_n, cols_n)
    for layer in range(2):
        w_in = dequantize(w_in_q[layer], exp_in[layer], BLK)
        w_out = dequantize(w_out_q[layer], exp_out[layer], BLK)
        pair = plain_update(
            layer, pair, row_mask, col_mask, norm_gain, norm_bias, w_in, w_out
        )
    return pair


PACK = 16


def swap_lanes(values):
    size = len(values)
    lanes = values[0].shape[-1]
    lane = lax.broadcasted_iota(jnp.int32, values[0].shape, 1)
    step = 1
    while step < size:
        low = (lane & step) == 0
        made = list(values)
        for v in range(size):
            if v & step == 0:
                a, b = values[v], values[v | step]
                made[v] = jnp.where(low, a, pltpu.roll(b, step, 1))
                made[v | step] = jnp.where(low, pltpu.roll(a, lanes - step, 1), b)
        values = made
        step *= 2
    return values


def norm_rows(values, gain, bias):
    average = jnp.mean(values, axis=-1, keepdims=True)
    centred = values - average
    variance = jnp.mean(centred * centred, axis=-1, keepdims=True)
    return (centred * lax.rsqrt(variance + EPS) * gain + bias).astype(jnp.bfloat16)


def scaled(q_ref, exp_ref, layer, first, count):
    width = q_ref.shape[1]
    per = 128 // BLK
    block = lax.broadcasted_iota(jnp.int32, (1, 128), 1) // BLK
    tiles = []
    for t in range(first, first + count):
        rows = []
        for rb in range(width // BLK):
            e = jnp.zeros((1, 128), jnp.int32)
            for s in range(per):
                e = jnp.where(block == s, exp_ref[layer, rb, t * per + s], e)
            q = q_ref[layer, rb * BLK : (rb + 1) * BLK, t * 128 : (t + 1) * 128]
            scale = jnp.exp2(e.astype(jnp.float32))
            rows.append((q.astype(jnp.float32) * scale).astype(jnp.bfloat16))
        tiles.append(jnp.concatenate(rows, axis=0))
    return jnp.concatenate(tiles, axis=1)


def gated(normed, weights, width):
    proj = jnp.dot(normed, weights, preferred_element_type=jnp.float32)
    p0, p1, p2, p3 = (proj[:, t * width : (t + 1) * width] for t in range(4))
    left = (jax.nn.sigmoid(p0) * p1).astype(jnp.bfloat16)
    right = (jax.nn.sigmoid(p2) * p3).astype(jnp.bfloat16)
    return left, right


def scatter_lanes(l_ref, r_ref, send_ref):
    size = send_ref.shape[0]
    outer = l_ref.shape[0] // size
    rows = l_ref.shape[1]
    for side, ref in enumerate((l_ref, r_ref)):
        for o in range(outer):
            for b in range(0, rows, PACK):
                got = swap_lanes([ref[o * size + v, b : b + PACK, :] for v in range(size)])
                at = (side * outer + o) * rows + b
                for d in range(size):
                    send_ref[d, at : at + PACK, :] = got[d]


def open_kernel(pair_ref, gain_ref, bias_ref, q_ref, exp_ref, send_ref, t_ref, l_ref, r_ref):
    rows_n, cols_n, width = pair_ref.shape
    weights = scaled(q_ref, exp_ref, 0, 0, 4)
    gain, bias = gain_ref[0, 0:1, :], bias_ref[0, 0:1, :]
    t_ref[...] = pair_ref[...].astype(jnp.float32)
    step = 8
    for k in range(0, cols_n, step):
        part = jnp.concatenate([t_ref[:, k + s, :] for s in range(step)], axis=0)
        left, right = gated(norm_rows(part, gain, bias), weights, width)
        l_ref[k : k + step] = left.reshape(step, rows_n, width)
        r_ref[k : k + step] = right.reshape(step, rows_n, width)
    scatter_lanes(l_ref, r_ref, send_ref)


def gate_kernel(layer, pair_ref, gain_ref, bias_ref, q_ref, exp_ref, gate_ref):
    rows_n, cols_n, width = pair_ref.shape
    weights = scaled(q_ref, exp_ref, layer, 4, 1)
    gain, bias = gain_ref[layer, 0:1, :], bias_ref[layer, 0:1, :]
    step = 16
    for i in range(0, rows_n, step):
        part = pair_ref[i : i + step].astype(jnp.float32).reshape(step * cols_n, width)
        proj = jnp.dot(
            norm_rows(part, gain, bias), weights, preferred_element_type=jnp.float32
        )
        gate_ref[i : i + step] = jax.nn.sigmoid(proj).reshape(step, cols_n, width)


def product_kernel(layer, row_count, own, got_ref, lane_ref, row_ref, x_ref):
    parts, both, lanes = got_ref.shape
    rows = both // 2
    col_count = parts // row_count
    size = lanes // own
    outer = rows // size
    tiles = lane_ref.shape[0]

    def tile(side, block, t):
        if layer == 0:
            r, h, c = block // outer, block % outer, t
        else:
            r, h, c = t // outer, t % outer, block
        at = side * rows + h * size
        return got_ref[r * col_count + c, at : at + size, :]

    group = lax.broadcasted_iota(jnp.int32, (1, lanes), 1) // size
    masks = [
        [jnp.where(group == a, lane_ref[t : t + 1, :], 0.0).astype(jnp.bfloat16) for t in range(tiles)]
        for a in range(own)
    ]
    right = jnp.concatenate(
        [
            jnp.concatenate([tile(1, block, t) for t in range(tiles)], axis=1)
            for block in range(tiles)
        ],
        axis=0,
    )
    for r in range(row_count):
        spread = []
        for h in range(outer):
            mine = [tile(0, r * outer + h, t) for t in range(tiles)]
            for a in range(own):
                spread.append(
                    jnp.concatenate([mine[t] * masks[a][t] for t in range(tiles)], axis=1)
                )
        left = jnp.concatenate(spread, axis=0)
        x = lax.dot_general(
            right, left, (((1,), (1,)), ((), ())), preferred_element_type=jnp.float32
        )
        for h in range(outer):
            block = r * outer + h
            piece = x[:, h * lanes : (h + 1) * lanes]
            piece = (piece * row_ref[...] * lane_ref[block : block + 1, :]).astype(jnp.bfloat16)
            for c in range(col_count):
                x_ref[r * col_count + c, h * size : (h + 1) * size, :] = piece[
                    c * size : (c + 1) * size, :
                ]


def gather_lanes(x_ref, u_ref):
    size = x_ref.shape[0]
    cols = u_ref.shape[1]
    outer = u_ref.shape[0] // size
    for o in range(outer):
        for b in range(0, cols, PACK):
            at = o * cols + b
            got = swap_lanes([x_ref[d, at : at + PACK, :] for d in range(size)])
            for v in range(size):
                u_ref[o * size + v, b : b + PACK, :] = got[v]


def finish_rows(layer, at, step, u_ref, pair_ref, gate_ref, gain_ref, bias_ref, w_out):
    _, cols_n, width = pair_ref.shape
    flat = (step * cols_n, width)
    x = u_ref[at : at + step].astype(jnp.float32).reshape(flat)
    y = norm_rows(x, gain_ref[layer, 1:2, :], bias_ref[layer, 1:2, :])
    update = jnp.dot(y, w_out, preferred_element_type=jnp.float32)
    base = pair_ref[at : at + step].astype(jnp.float32).reshape(flat)
    return (base + gate_ref[at : at + step].reshape(flat) * update).astype(jnp.bfloat16)


def middle_kernel(
    x_ref, pair_ref, gate_ref, gain_ref, bias_ref, q_ref, exp_ref, o_ref, oexp_ref,
    mid_ref, send_ref, u_ref, l_ref, r_ref,
):
    rows_n, cols_n, width = pair_ref.shape
    w_out = scaled(o_ref, oexp_ref, 0, 0, 1)
    weights = scaled(q_ref, exp_ref, 1, 0, 4)
    gain, bias = gain_ref[1, 0:1, :], bias_ref[1, 0:1, :]
    gather_lanes(x_ref, u_ref)
    step = 16
    for i in range(0, rows_n, step):
        mid = finish_rows(0, i, step, u_ref, pair_ref, gate_ref, gain_ref, bias_ref, w_out)
        mid_ref[i : i + step] = mid.reshape(step, cols_n, width)
        left, right = gated(norm_rows(mid.astype(jnp.float32), gain, bias), weights, width)
        l_ref[i : i + step] = left.reshape(step, cols_n, width)
        r_ref[i : i + step] = right.reshape(step, cols_n, width)
    scatter_lanes(l_ref, r_ref, send_ref)


def close_kernel(
    x_ref, pair_ref, gate_ref, gain_ref, bias_ref, o_ref, oexp_ref, out_ref, u_ref
):
    rows_n, cols_n, width = pair_ref.shape
    w_out = scaled(o_ref, oexp_ref, 1, 0, 1)
    gather_lanes(x_ref, u_ref)
    step = 16
    for i in range(0, rows_n, step):
        out = finish_rows(1, i, step, u_ref, pair_ref, gate_ref, gain_ref, bias_ref, w_out)
        out_ref[i : i + step] = out.reshape(step, cols_n, width)


VMEM = pl.BlockSpec(memory_space=pltpu.VMEM)
SMEM = pl.BlockSpec(memory_space=pltpu.SMEM)


def call(body, name, specs, outs, scratch, flops, moved):
    return pl.pallas_call(
        body,
        name=name,
        in_specs=specs,
        out_specs=jax.tree.map(lambda _: VMEM, outs),
        out_shape=outs,
        scratch_shapes=scratch,
        cost_estimate=pl.CostEstimate(flops=flops, bytes_accessed=moved, transcendentals=0),
        compiler_params=pltpu.CompilerParams(vmem_limit_bytes=40 * 2**20),
    )


def fast(pair, residue_mask, norm_gain, norm_bias, w_in_q, exp_in, w_out_q, exp_out):
    rows_n, cols_n, width = pair.shape
    row_count, col_count = lax.axis_size("row"), lax.axis_size("col")
    parts = row_count * col_count
    own = width // parts
    tokens = residue_mask.shape[0]
    bf16, f32 = jnp.bfloat16, jnp.float32
    mask = residue_mask.astype(f32)
    lane_mask = jnp.tile(mask.reshape(tokens // cols_n, cols_n), (1, own))
    row_mask = jnp.broadcast_to(mask[:, None], (tokens, width))

    block = (rows_n, cols_n, width)
    sent = jax.ShapeDtypeStruct((parts, 2 * rows_n, width), bf16)
    back = jax.ShapeDtypeStruct((parts, rows_n, width), bf16)
    pairs = rows_n * cols_n
    proj_cost = (2 * pairs * width * 4 * width, 8 * pairs * width)
    side = pltpu.VMEM(block, bf16)
    gate_out = jax.ShapeDtypeStruct(block, f32)

    def gate(layer, source):
        return call(
            functools.partial(gate_kernel, layer), f"gate{layer}",
            [VMEM, VMEM, VMEM, VMEM, SMEM], gate_out, [],
            2 * pairs * width * width, 8 * pairs * width,
        )(source, norm_gain, norm_bias, w_in_q, exp_in)

    def product(layer, got):
        return call(
            functools.partial(product_kernel, layer, row_count, own), f"product{layer}",
            [VMEM, VMEM, VMEM], back, [],
            2 * tokens * tokens * tokens * own * own, 6 * pairs * width,
        )(got, lane_mask, row_mask)

    def exchange(x):
        return lax.all_to_all(x, AXES, 0, 0, tiled=True)

    turned = pltpu.VMEM((cols_n, rows_n, width), bf16)
    send = call(
        open_kernel, "open", [VMEM, VMEM, VMEM, VMEM, SMEM], sent,
        [pltpu.VMEM(block, f32), turned, turned], *proj_cost,
    )(pair, norm_gain, norm_bias, w_in_q, exp_in)
    got = exchange(send)
    gate0 = gate(0, pair)
    x = exchange(product(0, got))
    mid, send = call(
        middle_kernel, "middle", [VMEM] * 6 + [SMEM, VMEM, SMEM],
        (jax.ShapeDtypeStruct(block, bf16), sent), [side, side, side], *proj_cost,
    )(x, pair, gate0, norm_gain, norm_bias, w_in_q, exp_in, w_out_q, exp_out)
    got = exchange(send)
    gate1 = gate(1, mid)
    x = exchange(product(1, got))
    return call(
        close_kernel, "close", [VMEM] * 6 + [SMEM],
        jax.ShapeDtypeStruct(block, bf16), [side], *proj_cost,
    )(x, mid, gate1, norm_gain, norm_bias, w_out_q, exp_out)


def solution(mesh):
    parts = mesh.shape["row"] * mesh.shape["col"]

    def shards(pair, *rest):
        rows_n, cols_n, width = pair.shape
        fits = (
            width == 128
            and width % parts == 0
            and cols_n == parts
            and rows_n % cols_n == 0
            and cols_n % PACK == 0
        )
        return (fast if fits else plain)(pair, *rest)

    placed = (P("row", "col", None), P(), P(), P(), P(), P(), P(), P())
    return jax.shard_map(
        shards, mesh=mesh, in_specs=placed, out_specs=P("row", "col", None), check_vma=False
    )
```

```python
import functools

import jax
import jax.numpy as jnp
from jax import lax
from jax.experimental import pallas as pl
from jax.experimental.pallas import tpu as pltpu
from jax.sharding import PartitionSpec as P

BLK = 32
AXES = ("row", "col")
EPS = 1e-05


def layer_norm(values, scale_vec, shift_vec):
    average = jnp.mean(values, axis=-1, keepdims=True)
    centred = values - average
    variance = jnp.mean(centred * centred, axis=-1, keepdims=True)
    return centred * lax.rsqrt(variance + EPS) * scale_vec + shift_vec


def dequantize(quantized, exponents, block_size):
    scales = jnp.exp2(exponents.astype(jnp.float32))
    scales = jnp.repeat(jnp.repeat(scales, block_size, axis=0), block_size, axis=1)
    return (quantized.astype(jnp.float32) * scales).astype(jnp.bfloat16)


def plain_update(layer, pair, row_mask, col_mask, norm_gain, norm_bias, w_in, w_out):
    rows_n, cols_n, width = pair.shape
    row_count, col_count = lax.axis_size("row"), lax.axis_size("col")
    parts = row_count * col_count
    own = width // parts
    normed = layer_norm(
        pair.astype(jnp.float32), norm_gain[layer, 0], norm_bias[layer, 0]
    ).astype(jnp.bfloat16)
    proj = jnp.einsum("ijc,cd->ijd", normed, w_in, preferred_element_type=jnp.float32)
    p0, p1, p2, p3, p4 = jnp.split(proj, 5, axis=-1)
    pm = (row_mask[:, None] * col_mask[None, :])[:, :, None]
    left = (jax.nn.sigmoid(p0) * p1 * pm).astype(jnp.bfloat16)
    right = (jax.nn.sigmoid(p2) * p3 * pm).astype(jnp.bfloat16)
    sent = jnp.stack([left, right]).reshape(2, rows_n, cols_n, parts, own)
    got = lax.all_to_all(sent.transpose(3, 0, 4, 1, 2), AXES, 0, 0, tiled=True)
    got = got.reshape(row_count, col_count, 2, own, rows_n, cols_n)
    whole = got.transpose(2, 3, 0, 4, 1, 5).reshape(
        2, own, row_count * rows_n, col_count * cols_n
    )
    spec = "cik,cjk->cij" if layer == 0 else "cki,ckj->cij"
    x = jnp.einsum(spec, whole[0], whole[1], preferred_element_type=jnp.float32)
    x = x.astype(jnp.bfloat16).reshape(own, row_count, rows_n, col_count, cols_n)
    back = x.transpose(1, 3, 0, 2, 4).reshape(parts, own, rows_n, cols_n)
    back = lax.all_to_all(back, AXES, 0, 0, tiled=True)
    x = back.transpose(2, 3, 0, 1).reshape(rows_n, cols_n, width)
    y = layer_norm(
        x.astype(jnp.float32), norm_gain[layer, 1], norm_bias[layer, 1]
    ).astype(jnp.bfloat16)
    out = jnp.einsum("ijc,cd->ijd", y, w_out, preferred_element_type=jnp.float32)
    return (pair.astype(jnp.float32) + jax.nn.sigmoid(p4) * out).astype(jnp.bfloat16)


def plain(pair, residue_mask, norm_gain, norm_bias, w_in_q, exp_in, w_out_q, exp_out):
    rows_n, cols_n, _ = pair.shape
    mask = residue_mask.astype(jnp.float32)
    row_mask = lax.dynamic_slice_in_dim(mask, lax.axis_index("row") * rows_n, rows_n)
    col_mask = lax.dynamic_slice_in_dim(mask, lax.axis_index("col") * cols_n, cols_n)
    for layer in range(2):
        w_in = dequantize(w_in_q[layer], exp_in[layer], BLK)
        w_out = dequantize(w_out_q[layer], exp_out[layer], BLK)
        pair = plain_update(
            layer, pair, row_mask, col_mask, norm_gain, norm_bias, w_in, w_out
        )
    return pair


PACK = 16


def pick_lanes(values, slot, back=False):
    size = len(values)
    lane = lax.broadcasted_iota(jnp.int32, values[0].shape, 1).astype(jnp.int16)
    step = 1
    while step < size:
        stay = (lane & jnp.int16(slot * step)) == 0
        move = -step if back else step
        values = [
            jnp.where(stay, values[v], values[(v + move) % size]) for v in range(size)
        ]
        step *= 2
    return values


def turn_lanes(value, by, size):
    if by == 0:
        return value
    lanes = value.shape[1]
    lane = lax.broadcasted_iota(jnp.int32, value.shape, 1).astype(jnp.int16)
    near = (lane & jnp.int16(size - 1)) < jnp.int16(size - by)
    return jnp.where(
        near, pltpu.roll(value, lanes - by, 1), pltpu.roll(value, size - by, 1)
    )


def twice(weights):
    none = jnp.zeros_like(weights)
    return jnp.concatenate(
        [
            jnp.concatenate([weights, none], axis=1),
            jnp.concatenate([none, weights], axis=1),
        ],
        axis=0,
    )


def beside(rows):
    half = rows.shape[0] // 2
    return jnp.concatenate([rows[:half], rows[half:]], axis=1)


def below(lanes):
    half = lanes.shape[1] // 2
    return jnp.concatenate([lanes[:, :half], lanes[:, half:]], axis=0)


def norm_beside(values, gain, bias):
    width = values.shape[1] // 2
    share = jnp.full((width, width), 1.0 / width, jnp.float32)
    row = lax.broadcasted_iota(jnp.int32, (width, width), 0)
    column = lax.broadcasted_iota(jnp.int32, (width, width), 1)
    centre = (row == column).astype(jnp.float32) - share
    centred = jnp.dot(
        values, twice(centre.astype(jnp.bfloat16)), preferred_element_type=jnp.float32
    )
    variance = jnp.dot(
        (centred * centred).astype(jnp.bfloat16),
        twice(share.astype(jnp.bfloat16)),
        preferred_element_type=jnp.float32,
    )
    gain = jnp.concatenate([gain, gain], axis=1)
    bias = jnp.concatenate([bias, bias], axis=1)
    return (centred * lax.rsqrt(variance + EPS) * gain + bias).astype(jnp.bfloat16)


def norm_rows(values, gain, bias):
    return below(norm_beside(beside(values), gain, bias))


def scaled(q_ref, exp_ref, layer, first, count):
    width = q_ref.shape[1]
    per = 128 // BLK
    block = lax.broadcasted_iota(jnp.int32, (1, 128), 1) // BLK
    tiles = []
    for t in range(first, first + count):
        rows = []
        for rb in range(width // BLK):
            e = jnp.zeros((1, 128), jnp.int32)
            for s in range(per):
                e = jnp.where(block == s, exp_ref[layer, rb, t * per + s], e)
            q = q_ref[layer, rb * BLK : (rb + 1) * BLK, t * 128 : (t + 1) * 128]
            scale = jnp.exp2(e.astype(jnp.float32))
            rows.append((q.astype(jnp.float32) * scale).astype(jnp.bfloat16))
        tiles.append(jnp.concatenate(rows, axis=0))
    return jnp.concatenate(tiles, axis=1)


def slotted(weights, width, size):
    slot = width // size
    row = lax.broadcasted_iota(jnp.int32, (width, width), 0)
    column = lax.broadcasted_iota(jnp.int32, (width, width), 1)
    order = (row == column % slot * size + column // slot).astype(jnp.bfloat16)
    tiles = [
        jnp.dot(
            weights[:, t : t + width], order, preferred_element_type=jnp.float32
        ).astype(jnp.bfloat16)
        for t in range(0, weights.shape[1], width)
    ]
    return jnp.concatenate(tiles, axis=1)


def gated(normed, weights, width):
    proj = jnp.dot(normed, weights, preferred_element_type=jnp.float32)
    p0, p1, p2, p3 = (proj[:, t * width : (t + 1) * width] for t in range(4))
    return jax.nn.sigmoid(p0) * p1, jax.nn.sigmoid(p2) * p3


def put_rolled(ref, at, values, rows, size):
    slot = values.shape[1] // size
    for s in range(values.shape[0] // rows):
        part = values[s * rows : (s + 1) * rows]
        shift = (at + s) % size * slot
        if shift:
            part = pltpu.roll(part, shift, 1)
        ref[at + s] = part.astype(jnp.bfloat16)


def scatter_lanes(l_ref, r_ref, send_ref):
    size = send_ref.shape[0]
    outer = l_ref.shape[0] // size
    rows = l_ref.shape[1]
    for side, ref in enumerate((l_ref, r_ref)):
        for o in range(outer):
            for b in range(0, rows, PACK):
                got = pick_lanes(
                    [ref[o * size + v, b : b + PACK, :] for v in range(size)],
                    ref.shape[2] // size,
                )
                at = (side * outer + o) * rows + b
                for d in range(size):
                    send_ref[d, at : at + PACK, :] = got[-d % size]


def open_kernel(
    pair_hbm, gain_hbm, bias_hbm, q_hbm, exp_hbm, send_ref,
    pair_ref, gain_ref, bias_ref, q_ref, exp_ref, t_ref, l_ref, r_ref, sems,
):
    moves = [
        pltpu.make_async_copy(source, target, sems.at[n])
        for n, (source, target) in enumerate(
            (
                (exp_hbm, exp_ref),
                (q_hbm, q_ref),
                (pair_hbm, pair_ref),
                (gain_hbm, gain_ref),
                (bias_hbm, bias_ref),
            )
        )
    ]
    for move in moves:
        move.start()
    for move in moves:
        move.wait()
    rows_n, cols_n, width = pair_ref.shape
    size = send_ref.shape[0]
    weights = slotted(scaled(q_ref, exp_ref, 0, 0, 4), width, size)
    gain, bias = gain_ref[0, 0:1, :], bias_ref[0, 0:1, :]
    t_ref[...] = pair_ref[...].astype(jnp.float32).reshape(t_ref.shape)
    step = 8
    for k in range(0, cols_n, step):
        part = jnp.concatenate(
            [t_ref[pl.ds(k + s, rows_n, stride=cols_n), :] for s in range(step)], axis=0
        )
        part = part.astype(jnp.bfloat16)
        left, right = gated(norm_rows(part, gain, bias), weights, width)
        put_rolled(l_ref, k, left, rows_n, size)
        put_rolled(r_ref, k, right, rows_n, size)
    scatter_lanes(l_ref, r_ref, send_ref)


def gate_kernel(layer, pair_ref, gain_ref, bias_ref, q_ref, exp_ref, gate_ref):
    rows_n, cols_n, width = pair_ref.shape
    weights = twice(scaled(q_ref, exp_ref, layer, 4, 1))
    gain, bias = gain_ref[layer, 0:1, :], bias_ref[layer, 0:1, :]
    step = 16
    for i in range(0, rows_n, step):
        part = beside(pair_ref[i : i + step].reshape(step * cols_n, width))
        proj = jnp.dot(
            norm_beside(part, gain, bias), weights, preferred_element_type=jnp.float32
        )
        gate_ref[i : i + step] = below(jax.nn.sigmoid(proj)).reshape(step, cols_n, width)


def product_kernel(
    layer, row_count, own, got_ref, sum_ref, lane_ref, row_ref, turn_ref, x_ref
):
    parts, both, lanes = got_ref.shape
    rows = both // 2
    col_count = parts // row_count
    size = lanes // own
    outer = rows // size
    tiles = lane_ref.shape[0]

    def tile(side, block, t):
        if layer == 0:
            r, h, c = block // outer, block % outer, t
        else:
            r, h, c = t // outer, t % outer, block
        at = side * rows + h * size
        return got_ref[r * col_count + c, at : at + size, :]

    channel = lax.broadcasted_iota(jnp.int32, (1, lanes), 1) % own
    masks = [
        [
            jnp.where(channel == a, sum_ref[t : t + 1, :], 0.0).astype(jnp.bfloat16)
            for t in range(tiles)
        ]
        for a in range(own)
    ]
    right = jnp.concatenate(
        [
            jnp.concatenate([tile(1, block, t) for t in range(tiles)], axis=1)
            for block in range(tiles)
        ],
        axis=0,
    )
    for r in range(row_count):
        spread = []
        for h in range(outer):
            mine = [tile(0, r * outer + h, t) for t in range(tiles)]
            for a in range(own):
                spread.append(
                    jnp.concatenate([mine[t] * masks[a][t] for t in range(tiles)], axis=1)
                )
        left = jnp.concatenate(spread, axis=0)
        x = lax.dot_general(
            right, left, (((1,), (1,)), ((), ())), preferred_element_type=jnp.float32
        )
        for h in range(outer):
            block = r * outer + h
            piece = x[:, h * lanes : (h + 1) * lanes]
            piece = piece * row_ref[...] * lane_ref[block : block + 1, :]
            turn = jnp.broadcast_to(turn_ref[...], piece.shape)
            piece = jnp.take_along_axis(piece, turn, axis=1, mode="promise_in_bounds")
            piece = piece.astype(jnp.bfloat16)
            for c in range(col_count):
                x_ref[r * col_count + c, h * size : (h + 1) * size, :] = piece[
                    c * size : (c + 1) * size, :
                ]


def gather_lanes(x_ref, u_ref):
    size = x_ref.shape[0]
    cols = u_ref.shape[1]
    outer = u_ref.shape[0] // size
    for o in range(outer):
        for b in range(0, cols, PACK):
            at = o * cols + b
            got = pick_lanes(
                [x_ref[-d % size, at : at + PACK, :] for d in range(size)], 1, True
            )
            for v in range(size):
                u_ref[o * size + v, b : b + PACK, :] = turn_lanes(got[v], v, size)


def finish_rows(layer, at, step, u_ref, pair_ref, gate_ref, gain_ref, bias_ref, w_out):
    _, cols_n, width = pair_ref.shape
    flat = (step * cols_n, width)
    x = beside(u_ref[at : at + step].reshape(flat))
    y = norm_beside(x, gain_ref[layer, 1:2, :], bias_ref[layer, 1:2, :])
    update = below(jnp.dot(y, w_out, preferred_element_type=jnp.float32))
    base = pair_ref[at : at + step].astype(jnp.float32).reshape(flat)
    return (base + gate_ref[at : at + step].reshape(flat) * update).astype(jnp.bfloat16)


def middle_kernel(
    x_ref, pair_ref, gate_ref, gain_ref, bias_ref, q_ref, exp_ref, o_ref, oexp_ref,
    mid_ref, send_ref, u_ref, l_ref, r_ref,
):
    rows_n, cols_n, width = pair_ref.shape
    w_out = twice(scaled(o_ref, oexp_ref, 0, 0, 1))
    size = send_ref.shape[0]
    weights = slotted(scaled(q_ref, exp_ref, 1, 0, 4), width, size)
    gain, bias = gain_ref[1, 0:1, :], bias_ref[1, 0:1, :]
    gather_lanes(x_ref, u_ref)
    step = 16
    for i in range(0, rows_n, step):
        mid = finish_rows(0, i, step, u_ref, pair_ref, gate_ref, gain_ref, bias_ref, w_out)
        mid_ref[i : i + step] = mid.reshape(step, cols_n, width)
        left, right = gated(norm_rows(mid, gain, bias), weights, width)
        put_rolled(l_ref, i, left, cols_n, size)
        put_rolled(r_ref, i, right, cols_n, size)
    scatter_lanes(l_ref, r_ref, send_ref)


def close_kernel(
    x_ref, pair_ref, gate_ref, gain_ref, bias_ref, o_ref, oexp_ref, out_ref, u_ref
):
    rows_n, cols_n, width = pair_ref.shape
    w_out = twice(scaled(o_ref, oexp_ref, 1, 0, 1))
    gather_lanes(x_ref, u_ref)
    step = 16
    for i in range(0, rows_n, step):
        out = finish_rows(1, i, step, u_ref, pair_ref, gate_ref, gain_ref, bias_ref, w_out)
        out_ref[i : i + step] = out.reshape(step, cols_n, width)


VMEM = pl.BlockSpec(memory_space=pltpu.VMEM)
SMEM = pl.BlockSpec(memory_space=pltpu.SMEM)
ANY = pl.BlockSpec(memory_space=pl.ANY)


def call(body, name, specs, outs, scratch, flops, moved):
    return pl.pallas_call(
        body,
        name=name,
        in_specs=specs,
        out_specs=jax.tree.map(lambda _: VMEM, outs),
        out_shape=outs,
        scratch_shapes=scratch,
        cost_estimate=pl.CostEstimate(flops=flops, bytes_accessed=moved, transcendentals=0),
        compiler_params=pltpu.CompilerParams(vmem_limit_bytes=40 * 2**20),
    )


def fast(pair, residue_mask, norm_gain, norm_bias, w_in_q, exp_in, w_out_q, exp_out):
    rows_n, cols_n, width = pair.shape
    row_count, col_count = lax.axis_size("row"), lax.axis_size("col")
    parts = row_count * col_count
    own = width // parts
    tokens = residue_mask.shape[0]
    bf16, f32 = jnp.bfloat16, jnp.float32
    mask = residue_mask.astype(f32)
    by_col = mask.reshape(tokens // cols_n, cols_n)
    lane_mask = jnp.tile(by_col, (1, own))
    here = lax.axis_index("row") * col_count + lax.axis_index("col")
    sum_mask = jnp.repeat(jnp.roll(by_col, here, axis=1), own, axis=1)
    lane = jnp.arange(width, dtype=jnp.int32)[None, :]
    turn = lane // parts * parts + (lane - here) % parts
    row_mask = jnp.broadcast_to(mask[:, None], (tokens, width))

    block = (rows_n, cols_n, width)
    sent = jax.ShapeDtypeStruct((parts, 2 * rows_n, width), bf16)
    back = jax.ShapeDtypeStruct((parts, rows_n, width), bf16)
    pairs = rows_n * cols_n
    proj_cost = (2 * pairs * width * 4 * width, 8 * pairs * width)
    side = pltpu.VMEM(block, bf16)
    gate_out = jax.ShapeDtypeStruct(block, f32)

    def gate(layer, source):
        return call(
            functools.partial(gate_kernel, layer), f"gate{layer}",
            [VMEM, VMEM, VMEM, VMEM, SMEM], gate_out, [],
            2 * pairs * width * width, 8 * pairs * width,
        )(source, norm_gain, norm_bias, w_in_q, exp_in)

    def product(layer, got):
        return call(
            functools.partial(product_kernel, layer, row_count, own), f"product{layer}",
            [VMEM] * 5, back, [],
            2 * tokens * tokens * tokens * own * own, 6 * pairs * width,
        )(got, sum_mask, lane_mask, row_mask, turn)

    def exchange(x):
        return lax.all_to_all(x, AXES, 0, 0, tiled=True)

    turned = pltpu.VMEM((cols_n, rows_n, width), bf16)
    send = call(
        open_kernel, "open", [ANY] * 5, sent,
        [
            side,
            pltpu.VMEM(norm_gain.shape, f32),
            pltpu.VMEM(norm_bias.shape, f32),
            pltpu.VMEM(w_in_q.shape, bf16),
            pltpu.SMEM(exp_in.shape, jnp.int32),
            pltpu.VMEM((rows_n * cols_n, width), f32),
            turned,
            turned,
            pltpu.SemaphoreType.DMA((5,)),
        ],
        *proj_cost,
    )(pair, norm_gain, norm_bias, w_in_q, exp_in)
    got = exchange(send)
    gate0 = gate(0, pair)
    x = exchange(product(0, got))
    mid, send = call(
        middle_kernel, "middle", [VMEM] * 6 + [SMEM, VMEM, SMEM],
        (jax.ShapeDtypeStruct(block, bf16), sent), [side, side, side], *proj_cost,
    )(x, pair, gate0, norm_gain, norm_bias, w_in_q, exp_in, w_out_q, exp_out)
    got = exchange(send)
    gate1 = gate(1, mid)
    x = exchange(product(1, got))
    return call(
        close_kernel, "close", [VMEM] * 6 + [SMEM],
        jax.ShapeDtypeStruct(block, bf16), [side], *proj_cost,
    )(x, mid, gate1, norm_gain, norm_bias, w_out_q, exp_out)


def solution(mesh):
    parts = mesh.shape["row"] * mesh.shape["col"]

    def shards(pair, *rest):
        rows_n, cols_n, width = pair.shape
        fits = (
            width == 128
            and width % parts == 0
            and cols_n == parts
            and rows_n % cols_n == 0
            and cols_n % PACK == 0
        )
        return (fast if fits else plain)(pair, *rest)

    placed = (P("row", "col", None), P(), P(), P(), P(), P(), P(), P())
    return jax.shard_map(
        shards, mesh=mesh, in_specs=placed, out_specs=P("row", "col", None), check_vma=False
    )
```

```python
import functools

import jax
import jax.numpy as jnp
from jax import lax
from jax.experimental import pallas as pl
from jax.experimental.pallas import tpu as pltpu
from jax.sharding import PartitionSpec as P

BLK = 32
AXES = ("row", "col")
EPS = 1e-05


def layer_norm(values, scale_vec, shift_vec):
    average = jnp.mean(values, axis=-1, keepdims=True)
    centred = values - average
    variance = jnp.mean(centred * centred, axis=-1, keepdims=True)
    return centred * lax.rsqrt(variance + EPS) * scale_vec + shift_vec


def dequantize(quantized, exponents, block_size):
    scales = jnp.exp2(exponents.astype(jnp.float32))
    scales = jnp.repeat(jnp.repeat(scales, block_size, axis=0), block_size, axis=1)
    return (quantized.astype(jnp.float32) * scales).astype(jnp.bfloat16)


def plain_update(layer, pair, row_mask, col_mask, norm_gain, norm_bias, w_in, w_out):
    rows_n, cols_n, width = pair.shape
    row_count, col_count = lax.axis_size("row"), lax.axis_size("col")
    parts = row_count * col_count
    own = width // parts
    normed = layer_norm(
        pair.astype(jnp.float32), norm_gain[layer, 0], norm_bias[layer, 0]
    ).astype(jnp.bfloat16)
    proj = jnp.einsum("ijc,cd->ijd", normed, w_in, preferred_element_type=jnp.float32)
    p0, p1, p2, p3, p4 = jnp.split(proj, 5, axis=-1)
    pm = (row_mask[:, None] * col_mask[None, :])[:, :, None]
    left = (jax.nn.sigmoid(p0) * p1 * pm).astype(jnp.bfloat16)
    right = (jax.nn.sigmoid(p2) * p3 * pm).astype(jnp.bfloat16)
    sent = jnp.stack([left, right]).reshape(2, rows_n, cols_n, parts, own)
    got = lax.all_to_all(sent.transpose(3, 0, 4, 1, 2), AXES, 0, 0, tiled=True)
    got = got.reshape(row_count, col_count, 2, own, rows_n, cols_n)
    whole = got.transpose(2, 3, 0, 4, 1, 5).reshape(
        2, own, row_count * rows_n, col_count * cols_n
    )
    spec = "cik,cjk->cij" if layer == 0 else "cki,ckj->cij"
    x = jnp.einsum(spec, whole[0], whole[1], preferred_element_type=jnp.float32)
    x = x.astype(jnp.bfloat16).reshape(own, row_count, rows_n, col_count, cols_n)
    back = x.transpose(1, 3, 0, 2, 4).reshape(parts, own, rows_n, cols_n)
    back = lax.all_to_all(back, AXES, 0, 0, tiled=True)
    x = back.transpose(2, 3, 0, 1).reshape(rows_n, cols_n, width)
    y = layer_norm(
        x.astype(jnp.float32), norm_gain[layer, 1], norm_bias[layer, 1]
    ).astype(jnp.bfloat16)
    out = jnp.einsum("ijc,cd->ijd", y, w_out, preferred_element_type=jnp.float32)
    return (pair.astype(jnp.float32) + jax.nn.sigmoid(p4) * out).astype(jnp.bfloat16)


def plain(pair, residue_mask, norm_gain, norm_bias, w_in_q, exp_in, w_out_q, exp_out):
    rows_n, cols_n, _ = pair.shape
    mask = residue_mask.astype(jnp.float32)
    row_mask = lax.dynamic_slice_in_dim(mask, lax.axis_index("row") * rows_n, rows_n)
    col_mask = lax.dynamic_slice_in_dim(mask, lax.axis_index("col") * cols_n, cols_n)
    for layer in range(2):
        w_in = dequantize(w_in_q[layer], exp_in[layer], BLK)
        w_out = dequantize(w_out_q[layer], exp_out[layer], BLK)
        pair = plain_update(
            layer, pair, row_mask, col_mask, norm_gain, norm_bias, w_in, w_out
        )
    return pair


PACK = 16


def pick_lanes(values, slot, back=False):
    size = len(values)
    lane = lax.broadcasted_iota(jnp.int32, values[0].shape, 1).astype(jnp.int16)
    step = 1
    while step < size:
        stay = (lane & jnp.int16(slot * step)) == 0
        move = -step if back else step
        values = [
            jnp.where(stay, values[v], values[(v + move) % size]) for v in range(size)
        ]
        step *= 2
    return values


def turn_lanes(value, by, size):
    if by == 0:
        return value
    lanes = value.shape[1]
    lane = lax.broadcasted_iota(jnp.int32, value.shape, 1).astype(jnp.int16)
    near = (lane & jnp.int16(size - 1)) < jnp.int16(size - by)
    return jnp.where(
        near, pltpu.roll(value, lanes - by, 1), pltpu.roll(value, size - by, 1)
    )


def twice(weights):
    none = jnp.zeros_like(weights)
    return jnp.concatenate(
        [
            jnp.concatenate([weights, none], axis=1),
            jnp.concatenate([none, weights], axis=1),
        ],
        axis=0,
    )


def beside(rows):
    half = rows.shape[0] // 2
    return jnp.concatenate([rows[:half], rows[half:]], axis=1)


def below(lanes):
    half = lanes.shape[1] // 2
    return jnp.concatenate([lanes[:, :half], lanes[:, half:]], axis=0)


def norm_beside(values, gain, bias):
    width = values.shape[1] // 2
    share = jnp.full((width, width), 1.0 / width, jnp.float32)
    row = lax.broadcasted_iota(jnp.int32, (width, width), 0)
    column = lax.broadcasted_iota(jnp.int32, (width, width), 1)
    centre = (row == column).astype(jnp.float32) - share
    centred = jnp.dot(
        values, twice(centre.astype(jnp.bfloat16)), preferred_element_type=jnp.float32
    )
    variance = jnp.dot(
        (centred * centred).astype(jnp.bfloat16),
        twice(share.astype(jnp.bfloat16)),
        preferred_element_type=jnp.float32,
    )
    gain = jnp.concatenate([gain, gain], axis=1)
    bias = jnp.concatenate([bias, bias], axis=1)
    return (centred * lax.rsqrt(variance + EPS) * gain + bias).astype(jnp.bfloat16)


def norm_rows(values, gain, bias):
    return below(norm_beside(beside(values), gain, bias))


def scaled(q_ref, exp_ref, layer, first, count):
    width = q_ref.shape[1]
    per = 128 // BLK
    block = lax.broadcasted_iota(jnp.int32, (1, 128), 1) // BLK
    tiles = []
    for t in range(first, first + count):
        rows = []
        for rb in range(width // BLK):
            e = jnp.zeros((1, 128), jnp.int32)
            for s in range(per):
                e = jnp.where(block == s, exp_ref[layer, rb, t * per + s], e)
            q = q_ref[layer, rb * BLK : (rb + 1) * BLK, t * 128 : (t + 1) * 128]
            scale = jnp.exp2(e.astype(jnp.float32))
            rows.append((q.astype(jnp.float32) * scale).astype(jnp.bfloat16))
        tiles.append(jnp.concatenate(rows, axis=0))
    return jnp.concatenate(tiles, axis=1)


def slotted(weights, width, size):
    slot = width // size
    row = lax.broadcasted_iota(jnp.int32, (width, width), 0)
    column = lax.broadcasted_iota(jnp.int32, (width, width), 1)
    order = (row == column % slot * size + column // slot).astype(jnp.bfloat16)
    tiles = [
        jnp.dot(
            weights[:, t : t + width], order, preferred_element_type=jnp.float32
        ).astype(jnp.bfloat16)
        for t in range(0, weights.shape[1], width)
    ]
    return jnp.concatenate(tiles, axis=1)


def gated(normed, weights, width):
    proj = jnp.dot(normed, weights, preferred_element_type=jnp.float32)
    p0, p1, p2, p3 = (proj[:, t * width : (t + 1) * width] for t in range(4))
    return jax.nn.sigmoid(p0) * p1, jax.nn.sigmoid(p2) * p3


def put_rolled(ref, at, values, rows, size):
    slot = values.shape[1] // size
    for s in range(values.shape[0] // rows):
        part = values[s * rows : (s + 1) * rows]
        shift = (at + s) % size * slot
        if shift:
            part = pltpu.roll(part, shift, 1)
        ref[at + s] = part.astype(jnp.bfloat16)


def scatter_lanes(l_ref, r_ref, send_ref):
    size = send_ref.shape[0]
    outer = l_ref.shape[0] // size
    rows = l_ref.shape[1]
    for side, ref in enumerate((l_ref, r_ref)):
        for o in range(outer):
            for b in range(0, rows, PACK):
                got = pick_lanes(
                    [ref[o * size + v, b : b + PACK, :] for v in range(size)],
                    ref.shape[2] // size,
                )
                at = (side * outer + o) * rows + b
                for d in range(size):
                    send_ref[d, at : at + PACK, :] = got[-d % size]


OPEN_STEP = 16


CLOSE_STEP = 32


def in_turn(count, first, second):
    ready = first(0)
    for n in range(count):
        following = first(n + 1) if n + 1 < count else None
        second(n, ready)
        ready = following


def open_kernel(
    pair_hbm, gain_hbm, bias_hbm, q_hbm, exp_hbm, send_ref,
    pair_ref, gain_ref, bias_ref, q_ref, exp_ref, t_ref, l_ref, r_ref, sems,
):
    moves = [
        pltpu.make_async_copy(source, target, sems.at[n])
        for n, (source, target) in enumerate(
            (
                (exp_hbm, exp_ref),
                (q_hbm.at[0:1, :, 0 : q_ref.shape[2]], q_ref),
                (gain_hbm, gain_ref),
                (bias_hbm, bias_ref),
                (pair_hbm, pair_ref),
            )
        )
    ]
    for move in moves:
        move.start()
    for move in moves[:-1]:
        move.wait()
    rows_n, cols_n, width = pair_ref.shape
    size = send_ref.shape[0]
    weights = slotted(scaled(q_ref, exp_ref, 0, 0, 4), width, size)
    gain, bias = gain_ref[0, 0:1, :], bias_ref[0, 0:1, :]
    moves[-1].wait()
    t_ref[...] = pair_ref[...].astype(jnp.float32).reshape(t_ref.shape)
    step = OPEN_STEP

    def norm(n):
        part = jnp.concatenate(
            [
                t_ref[pl.ds(n * step + s, rows_n, stride=cols_n), :]
                for s in range(step)
            ],
            axis=0,
        )
        return norm_rows(part.astype(jnp.bfloat16), gain, bias)

    def project(n, normed):
        left, right = gated(normed, weights, width)
        put_rolled(l_ref, n * step, left, rows_n, size)
        put_rolled(r_ref, n * step, right, rows_n, size)

    in_turn(cols_n // step, norm, project)
    scatter_lanes(l_ref, r_ref, send_ref)


def gate_kernel(
    layer, size, pair_ref, gain_ref, bias_ref, q_ref, exp_ref, o_ref, oexp_ref,
    gate_ref, out_ref, *next_ref,
):
    rows_n, cols_n, width = pair_ref.shape
    weights = twice(scaled(q_ref, exp_ref, layer, 4, 1))
    gain, bias = gain_ref[layer, 0:1, :], bias_ref[layer, 0:1, :]
    out_ref[...] = twice(scaled(o_ref, oexp_ref, layer, 0, 1))
    if next_ref:
        next_ref[0][...] = slotted(scaled(q_ref, exp_ref, layer + 1, 0, 4), width, size)
    step = 16
    for i in range(0, rows_n, step):
        part = beside(pair_ref[i : i + step].reshape(step * cols_n, width))
        proj = jnp.dot(
            norm_beside(part, gain, bias), weights, preferred_element_type=jnp.float32
        )
        gate_ref[i : i + step] = below(jax.nn.sigmoid(proj)).reshape(step, cols_n, width)


def product_kernel(
    layer, row_count, own, got_ref, sum_ref, lane_ref, row_ref, turn_ref, x_ref
):
    parts, both, lanes = got_ref.shape
    rows = both // 2
    col_count = parts // row_count
    size = lanes // own
    outer = rows // size
    tiles = lane_ref.shape[0]

    def tile(side, block, t):
        if layer == 0:
            r, h, c = block // outer, block % outer, t
        else:
            r, h, c = t // outer, t % outer, block
        at = side * rows + h * size
        return got_ref[r * col_count + c, at : at + size, :]

    channel = lax.broadcasted_iota(jnp.int32, (1, lanes), 1) % own
    masks = [
        [
            jnp.where(channel == a, sum_ref[t : t + 1, :], 0.0).astype(jnp.bfloat16)
            for t in range(tiles)
        ]
        for a in range(own)
    ]
    right = jnp.concatenate(
        [
            jnp.concatenate([tile(1, block, t) for t in range(tiles)], axis=1)
            for block in range(tiles)
        ],
        axis=0,
    )
    for r in range(row_count):
        spread = []
        for h in range(outer):
            mine = [tile(0, r * outer + h, t) for t in range(tiles)]
            for a in range(own):
                spread.append(
                    jnp.concatenate([mine[t] * masks[a][t] for t in range(tiles)], axis=1)
                )
        left = jnp.concatenate(spread, axis=0)
        x = lax.dot_general(
            right, left, (((1,), (1,)), ((), ())), preferred_element_type=jnp.float32
        )
        for h in range(outer):
            block = r * outer + h
            piece = x[:, h * lanes : (h + 1) * lanes]
            piece = piece * row_ref[...] * lane_ref[block : block + 1, :]
            turn = jnp.broadcast_to(turn_ref[...], piece.shape)
            piece = jnp.take_along_axis(piece, turn, axis=1, mode="promise_in_bounds")
            piece = piece.astype(jnp.bfloat16)
            for c in range(col_count):
                x_ref[r * col_count + c, h * size : (h + 1) * size, :] = piece[
                    c * size : (c + 1) * size, :
                ]


def gather_lanes(x_ref, u_ref):
    size = x_ref.shape[0]
    cols = u_ref.shape[1]
    outer = u_ref.shape[0] // size
    for o in range(outer):
        for b in range(0, cols, PACK):
            at = o * cols + b
            got = pick_lanes(
                [x_ref[-d % size, at : at + PACK, :] for d in range(size)], 1, True
            )
            for v in range(size):
                u_ref[o * size + v, b : b + PACK, :] = turn_lanes(got[v], v, size)


def finish_rows(layer, at, step, u_ref, pair_ref, gate_ref, gain_ref, bias_ref, w_out):
    _, cols_n, width = pair_ref.shape
    flat = (step * cols_n, width)
    x = beside(u_ref[at : at + step].reshape(flat))
    y = norm_beside(x, gain_ref[layer, 1:2, :], bias_ref[layer, 1:2, :])
    update = below(jnp.dot(y, w_out, preferred_element_type=jnp.float32))
    base = pair_ref[at : at + step].astype(jnp.float32).reshape(flat)
    return (base + gate_ref[at : at + step].reshape(flat) * update).astype(jnp.bfloat16)


def middle_kernel(
    x_ref, pair_ref, gate_ref, w_out_ref, w_in_ref, gain_ref, bias_ref,
    mid_ref, send_ref, u_ref, l_ref, r_ref,
):
    rows_n, cols_n, width = pair_ref.shape
    size = send_ref.shape[0]
    gather_lanes(x_ref, u_ref)
    mid = finish_rows(
        0, 0, rows_n, u_ref, pair_ref, gate_ref, gain_ref, bias_ref, w_out_ref[...]
    )
    mid_ref[...] = mid.reshape(rows_n, cols_n, width)
    normed = norm_rows(mid, gain_ref[1, 0:1, :], bias_ref[1, 0:1, :])
    left, right = gated(normed, w_in_ref[...], width)
    put_rolled(l_ref, 0, left, cols_n, size)
    put_rolled(r_ref, 0, right, cols_n, size)
    scatter_lanes(l_ref, r_ref, send_ref)


def close_kernel(
    x_ref, pair_ref, gate_ref, w_out_ref, gain_ref, bias_ref, out_ref, u_ref
):
    rows_n, cols_n, width = pair_ref.shape
    gather_lanes(x_ref, u_ref)
    step = CLOSE_STEP
    for i in range(0, rows_n, step):
        out = finish_rows(
            1, i, step, u_ref, pair_ref, gate_ref, gain_ref, bias_ref, w_out_ref[...]
        )
        out_ref[i : i + step] = out.reshape(step, cols_n, width)


VMEM = pl.BlockSpec(memory_space=pltpu.VMEM)
SMEM = pl.BlockSpec(memory_space=pltpu.SMEM)
HBM = pl.BlockSpec(memory_space=pltpu.HBM)


def call(body, name, specs, outs, scratch, flops, moved, grant=40 * 2**20):
    return pl.pallas_call(
        body,
        name=name,
        in_specs=specs,
        out_specs=jax.tree.map(lambda _: VMEM, outs),
        out_shape=outs,
        scratch_shapes=scratch,
        cost_estimate=pl.CostEstimate(flops=flops, bytes_accessed=moved, transcendentals=0),
        compiler_params=pltpu.CompilerParams(vmem_limit_bytes=grant),
    )


def fast(pair, residue_mask, norm_gain, norm_bias, w_in_q, exp_in, w_out_q, exp_out):
    rows_n, cols_n, width = pair.shape
    row_count, col_count = lax.axis_size("row"), lax.axis_size("col")
    parts = row_count * col_count
    own = width // parts
    tokens = residue_mask.shape[0]
    bf16, f32 = jnp.bfloat16, jnp.float32
    mask = residue_mask.astype(f32)
    by_col = mask.reshape(tokens // cols_n, cols_n)
    lane_mask = jnp.tile(by_col, (1, own))
    here = lax.axis_index("row") * col_count + lax.axis_index("col")
    sum_mask = jnp.repeat(jnp.roll(by_col, here, axis=1), own, axis=1)
    lane = jnp.arange(width, dtype=jnp.int32)[None, :]
    turn = lane // parts * parts + (lane - here) % parts
    row_mask = jnp.broadcast_to(mask[:, None], (tokens, width))

    block = (rows_n, cols_n, width)
    sent = jax.ShapeDtypeStruct((parts, 2 * rows_n, width), bf16)
    back = jax.ShapeDtypeStruct((parts, rows_n, width), bf16)
    pairs = rows_n * cols_n
    proj_cost = (2 * pairs * width * 4 * width, 8 * pairs * width)
    side = pltpu.VMEM(block, bf16)
    gate_outs = (
        jax.ShapeDtypeStruct(block, f32),
        jax.ShapeDtypeStruct((2 * width, 2 * width), bf16),
        jax.ShapeDtypeStruct((width, 4 * width), bf16),
    )

    def gate(layer, source):
        return call(
            functools.partial(gate_kernel, layer, parts), f"gate{layer}",
            [VMEM, VMEM, VMEM, VMEM, SMEM, VMEM, SMEM], gate_outs[: 3 - layer], [],
            2 * pairs * width * width, 8 * pairs * width,
        )(source, norm_gain, norm_bias, w_in_q, exp_in, w_out_q, exp_out)

    def product(layer, got):
        return call(
            functools.partial(product_kernel, layer, row_count, own), f"product{layer}",
            [VMEM] * 5, back, [],
            2 * tokens * tokens * tokens * own * own, 6 * pairs * width,
        )(got, sum_mask, lane_mask, row_mask, turn)

    def exchange(x):
        return lax.all_to_all(x, AXES, 0, 0, tiled=True)

    turned = pltpu.VMEM((cols_n, rows_n, width), bf16)
    send = call(
        open_kernel, "open", [HBM] * 5, sent,
        [
            side,
            pltpu.VMEM(norm_gain.shape, f32),
            pltpu.VMEM(norm_bias.shape, f32),
            pltpu.VMEM((1, width, 4 * width), bf16),
            pltpu.SMEM(exp_in.shape, jnp.int32),
            pltpu.VMEM((rows_n * cols_n, width), f32),
            turned,
            turned,
            pltpu.SemaphoreType.DMA((5,)),
        ],
        *proj_cost, grant=None,
    )(pair, norm_gain, norm_bias, w_in_q, exp_in)
    got = exchange(send)
    gate0, w_out, w_in = gate(0, pair)
    x = exchange(product(0, got))
    mid, send = call(
        middle_kernel, "middle", [VMEM] * 7,
        (jax.ShapeDtypeStruct(block, bf16), sent), [side, side, side], *proj_cost,
    )(x, pair, gate0, w_out, w_in, norm_gain, norm_bias)
    got = exchange(send)
    gate1, w_out = gate(1, mid)
    x = exchange(product(1, got))
    return call(
        close_kernel, "close", [VMEM] * 6,
        jax.ShapeDtypeStruct(block, bf16), [side], *proj_cost,
    )(x, mid, gate1, w_out, norm_gain, norm_bias)


def solution(mesh):
    parts = mesh.shape["row"] * mesh.shape["col"]

    def shards(pair, *rest):
        rows_n, cols_n, width = pair.shape
        fits = (
            width == 128
            and width % parts == 0
            and cols_n == parts
            and rows_n % cols_n == 0
            and cols_n % PACK == 0
        )
        return (fast if fits else plain)(pair, *rest)

    placed = (P("row", "col", None), P(), P(), P(), P(), P(), P(), P())
    return jax.shard_map(
        shards, mesh=mesh, in_specs=placed, out_specs=P("row", "col", None), check_vma=False
    )
```

```python
import functools

import jax
import jax.numpy as jnp
from jax import lax
from jax.experimental import pallas as pl
from jax.experimental.pallas import tpu as pltpu
from jax.sharding import PartitionSpec as P

BLK = 32
AXES = ("row", "col")
EPS = 1e-05


def layer_norm(values, scale_vec, shift_vec):
    average = jnp.mean(values, axis=-1, keepdims=True)
    centred = values - average
    variance = jnp.mean(centred * centred, axis=-1, keepdims=True)
    return centred * lax.rsqrt(variance + EPS) * scale_vec + shift_vec


def dequantize(quantized, exponents, block_size):
    scales = jnp.exp2(exponents.astype(jnp.float32))
    scales = jnp.repeat(jnp.repeat(scales, block_size, axis=0), block_size, axis=1)
    return (quantized.astype(jnp.float32) * scales).astype(jnp.bfloat16)


def plain_update(layer, pair, row_mask, col_mask, norm_gain, norm_bias, w_in, w_out):
    rows_n, cols_n, width = pair.shape
    row_count, col_count = lax.axis_size("row"), lax.axis_size("col")
    parts = row_count * col_count
    own = width // parts
    normed = layer_norm(
        pair.astype(jnp.float32), norm_gain[layer, 0], norm_bias[layer, 0]
    ).astype(jnp.bfloat16)
    proj = jnp.einsum("ijc,cd->ijd", normed, w_in, preferred_element_type=jnp.float32)
    p0, p1, p2, p3, p4 = jnp.split(proj, 5, axis=-1)
    pm = (row_mask[:, None] * col_mask[None, :])[:, :, None]
    left = (jax.nn.sigmoid(p0) * p1 * pm).astype(jnp.bfloat16)
    right = (jax.nn.sigmoid(p2) * p3 * pm).astype(jnp.bfloat16)
    sent = jnp.stack([left, right]).reshape(2, rows_n, cols_n, parts, own)
    got = lax.all_to_all(sent.transpose(3, 0, 4, 1, 2), AXES, 0, 0, tiled=True)
    got = got.reshape(row_count, col_count, 2, own, rows_n, cols_n)
    whole = got.transpose(2, 3, 0, 4, 1, 5).reshape(
        2, own, row_count * rows_n, col_count * cols_n
    )
    spec = "cik,cjk->cij" if layer == 0 else "cki,ckj->cij"
    x = jnp.einsum(spec, whole[0], whole[1], preferred_element_type=jnp.float32)
    x = x.astype(jnp.bfloat16).reshape(own, row_count, rows_n, col_count, cols_n)
    back = x.transpose(1, 3, 0, 2, 4).reshape(parts, own, rows_n, cols_n)
    back = lax.all_to_all(back, AXES, 0, 0, tiled=True)
    x = back.transpose(2, 3, 0, 1).reshape(rows_n, cols_n, width)
    y = layer_norm(
        x.astype(jnp.float32), norm_gain[layer, 1], norm_bias[layer, 1]
    ).astype(jnp.bfloat16)
    out = jnp.einsum("ijc,cd->ijd", y, w_out, preferred_element_type=jnp.float32)
    return (pair.astype(jnp.float32) + jax.nn.sigmoid(p4) * out).astype(jnp.bfloat16)


def plain(pair, residue_mask, norm_gain, norm_bias, w_in_q, exp_in, w_out_q, exp_out):
    rows_n, cols_n, _ = pair.shape
    mask = residue_mask.astype(jnp.float32)
    row_mask = lax.dynamic_slice_in_dim(mask, lax.axis_index("row") * rows_n, rows_n)
    col_mask = lax.dynamic_slice_in_dim(mask, lax.axis_index("col") * cols_n, cols_n)
    for layer in range(2):
        w_in = dequantize(w_in_q[layer], exp_in[layer], BLK)
        w_out = dequantize(w_out_q[layer], exp_out[layer], BLK)
        pair = plain_update(
            layer, pair, row_mask, col_mask, norm_gain, norm_bias, w_in, w_out
        )
    return pair


PACK = 16


def pick_lanes(values, slot, back=False):
    size = len(values)
    lane = lax.broadcasted_iota(jnp.int32, values[0].shape, 1).astype(jnp.int16)
    step = 1
    while step < size:
        stay = (lane & jnp.int16(slot * step)) == 0
        move = -step if back else step
        values = [
            jnp.where(stay, values[v], values[(v + move) % size]) for v in range(size)
        ]
        step *= 2
    return values


def turn_lanes(value, by, size):
    if by == 0:
        return value
    lanes = value.shape[1]
    lane = lax.broadcasted_iota(jnp.int32, value.shape, 1).astype(jnp.int16)
    near = (lane & jnp.int16(size - 1)) < jnp.int16(size - by)
    return jnp.where(
        near, pltpu.roll(value, lanes - by, 1), pltpu.roll(value, size - by, 1)
    )


def twice(weights):
    none = jnp.zeros_like(weights)
    return jnp.concatenate(
        [
            jnp.concatenate([weights, none], axis=1),
            jnp.concatenate([none, weights], axis=1),
        ],
        axis=0,
    )


def beside(rows):
    half = rows.shape[0] // 2
    return jnp.concatenate([rows[:half], rows[half:]], axis=1)


def below(lanes):
    half = lanes.shape[1] // 2
    return jnp.concatenate([lanes[:, :half], lanes[:, half:]], axis=0)


def norm_beside(values, gain, bias):
    width = values.shape[1] // 2
    share = jnp.full((width, width), 1.0 / width, jnp.float32)
    row = lax.broadcasted_iota(jnp.int32, (width, width), 0)
    column = lax.broadcasted_iota(jnp.int32, (width, width), 1)
    centre = (row == column).astype(jnp.float32) - share
    centred = jnp.dot(
        values, twice(centre.astype(jnp.bfloat16)), preferred_element_type=jnp.float32
    )
    variance = jnp.dot(
        (centred * centred).astype(jnp.bfloat16),
        twice(share.astype(jnp.bfloat16)),
        preferred_element_type=jnp.float32,
    )
    gain = jnp.concatenate([gain, gain], axis=1)
    bias = jnp.concatenate([bias, bias], axis=1)
    return (centred * lax.rsqrt(variance + EPS) * gain + bias).astype(jnp.bfloat16)


def norm_rows(values, gain, bias):
    return below(norm_beside(beside(values), gain, bias))


def scaled(q_ref, exp_ref, layer, first, count, ahead=0):
    width = q_ref.shape[1]
    per = 128 // BLK
    block = lax.broadcasted_iota(jnp.int32, (1, 128), 1) // BLK
    tiles = []
    for t in range(first, first + count):
        rows = []
        for rb in range(width // BLK):
            e = jnp.zeros((1, 128), jnp.int32)
            for s in range(per):
                e = jnp.where(block == s, exp_ref[layer, rb, (ahead + t) * per + s], e)
            q = q_ref[layer, rb * BLK : (rb + 1) * BLK, t * 128 : (t + 1) * 128]
            scale = jnp.exp2(e.astype(jnp.float32))
            rows.append((q.astype(jnp.float32) * scale).astype(jnp.bfloat16))
        tiles.append(jnp.concatenate(rows, axis=0))
    return jnp.concatenate(tiles, axis=1)


def slotted(weights, width, size):
    slot = width // size
    row = lax.broadcasted_iota(jnp.int32, (width, width), 0)
    column = lax.broadcasted_iota(jnp.int32, (width, width), 1)
    order = (row == column % slot * size + column // slot).astype(jnp.bfloat16)
    tiles = [
        jnp.dot(
            weights[:, t : t + width], order, preferred_element_type=jnp.float32
        ).astype(jnp.bfloat16)
        for t in range(0, weights.shape[1], width)
    ]
    return jnp.concatenate(tiles, axis=1)


def gated(normed, weights, width):
    proj = jnp.dot(normed, weights, preferred_element_type=jnp.float32)
    return [
        jax.nn.sigmoid(proj[:, t : t + width]) * proj[:, t + width : t + 2 * width]
        for t in range(0, proj.shape[1], 2 * width)
    ]


def put_rolled(ref, at, values, rows, size):
    slot = values.shape[1] // size
    for s in range(values.shape[0] // rows):
        part = values[s * rows : (s + 1) * rows]
        shift = (at + s) % size * slot
        if shift:
            part = pltpu.roll(part, shift, 1)
        ref[at + s] = part.astype(jnp.bfloat16)


def scatter_lanes(ref, size, put):
    rows = ref.shape[1]
    for o in range(ref.shape[0] // size):
        for b in range(0, rows, PACK):
            got = pick_lanes(
                [ref[o * size + v, b : b + PACK, :] for v in range(size)],
                ref.shape[2] // size,
            )
            for d in range(size):
                put(d, o * rows + b, got[-d % size])


OPEN_STEP = 16


CLOSE_STEP = 32


def in_turn(count, first, second):
    ready = first(0)
    for n in range(count):
        following = first(n + 1) if n + 1 < count else None
        second(n, ready)
        ready = following


def operand(size, pair_ref, gain_ref, bias_ref, weights, t_ref, v_ref):
    rows_n, cols_n, width = pair_ref.shape
    gain, bias = gain_ref[0, 0:1, :], bias_ref[0, 0:1, :]
    t_ref[...] = pair_ref[...].astype(jnp.float32).reshape(t_ref.shape)
    step = OPEN_STEP

    def norm(n):
        part = jnp.concatenate(
            [
                t_ref[pl.ds(n * step + s, rows_n, stride=cols_n), :]
                for s in range(step)
            ],
            axis=0,
        )
        return norm_rows(part.astype(jnp.bfloat16), gain, bias)

    def project(n, normed):
        (made,) = gated(normed, weights, width)
        put_rolled(v_ref, n * step, made, rows_n, size)

    in_turn(cols_n // step, norm, project)


def right_kernel(
    pair_hbm, gain_hbm, bias_hbm, q_hbm, exp_hbm, send_ref, gain0_ref,
    pair_ref, gain_ref, bias_ref, q_ref, exp_ref, t_ref, v_ref, sems,
):
    first = q_ref.shape[2]
    moves = [
        pltpu.make_async_copy(source, target, sems.at[n])
        for n, (source, target) in enumerate(
            (
                (exp_hbm, exp_ref),
                (q_hbm.at[0:1, :, first : 2 * first], q_ref),
                (gain_hbm, gain_ref),
                (bias_hbm, bias_ref),
                (pair_hbm, pair_ref),
            )
        )
    ]
    for move in moves:
        move.start()
    for move in moves[:-1]:
        move.wait()
    width = pair_ref.shape[2]
    size = send_ref.shape[0]
    near = size // 2
    weights = slotted(scaled(q_ref, exp_ref, 0, 0, 2, 2), width, size)
    moves[-1].wait()
    gain0_ref[...] = gain_ref[...]
    operand(size, pair_ref, gain_ref, bias_ref, weights, t_ref, v_ref)
    rows = v_ref.shape[1]

    def put(d, at, part):
        at = d % 2 * rows + at
        send_ref[d // 2, at : at + PACK, :] = part
        send_ref[near + d // 2, at : at + PACK, :] = part

    scatter_lanes(v_ref, size, put)


def left_kernel(
    here_ref, pair_ref, gain_ref, bias_ref, q_ref, exp_ref, *refs
):
    *outs, t_ref, v_ref, o_ref = refs
    width = pair_ref.shape[2]
    size = 2 * o_ref.shape[0]
    weights = slotted(scaled(q_ref, exp_ref, 0, 0, 2), width, size)
    operand(size, pair_ref, gain_ref, bias_ref, weights, t_ref, v_ref)
    rows = v_ref.shape[1]
    here = here_ref[0]

    def put(d, at, part):
        at = d % 2 * rows + at
        o_ref[here ^ (d // 2), at : at + PACK, :] = part

    scatter_lanes(v_ref, size, put)
    for n, out in enumerate(outs):
        out[...] = o_ref[2 * n : 2 * n + 2]


def gate_kernel(
    layer, size, pair_ref, gain_ref, bias_ref, q_ref, exp_ref, o_ref, oexp_ref,
    gate_ref, out_ref, *next_ref,
):
    rows_n, cols_n, width = pair_ref.shape
    weights = twice(scaled(q_ref, exp_ref, layer, 4, 1))
    gain, bias = gain_ref[layer, 0:1, :], bias_ref[layer, 0:1, :]
    out_ref[...] = twice(scaled(o_ref, oexp_ref, layer, 0, 1))
    if next_ref:
        next_ref[0][...] = slotted(scaled(q_ref, exp_ref, layer + 1, 0, 4), width, size)
    step = 16
    for i in range(0, rows_n, step):
        part = beside(pair_ref[i : i + step].reshape(step * cols_n, width))
        proj = jnp.dot(
            norm_beside(part, gain, bias), weights, preferred_element_type=jnp.float32
        )
        gate_ref[i : i + step] = below(jax.nn.sigmoid(proj)).reshape(step, cols_n, width)


def channel_masks(sum_ref, own, lanes):
    channel = lax.broadcasted_iota(jnp.int32, (1, lanes), 1) % own
    return [
        [
            jnp.where(channel == a, sum_ref[t : t + 1, :], 0.0).astype(jnp.bfloat16)
            for t in range(sum_ref.shape[0])
        ]
        for a in range(own)
    ]


def multiply(right, blocks, masks, row_ref, lane_rows, group, size, put):
    lanes = blocks[0][0].shape[1]
    lane = lax.broadcasted_iota(jnp.int32, (1, lanes), 1)
    turn = (lane & -size) + ((lane - group) & (size - 1))
    turn = jnp.broadcast_to(turn, (right.shape[0], lanes))
    left = jnp.concatenate(
        [
            jnp.concatenate([part * mask for part, mask in zip(parts, row)], axis=1)
            for parts in blocks
            for row in masks
        ],
        axis=0,
    )
    x = lax.dot_general(
        right, left, (((1,), (1,)), ((), ())), preferred_element_type=jnp.float32
    )
    for h in range(len(blocks)):
        piece = x[:, h * lanes : (h + 1) * lanes] * row_ref[...] * lane_rows[h]
        piece = jnp.take_along_axis(piece, turn, axis=1, mode="promise_in_bounds")
        put(h, piece.astype(jnp.bfloat16))


def product0_kernel(
    row_count, own, here_ref, right_ref, sum_ref, lane_ref, row_ref, *refs
):
    *near_refs, far_ref, x_ref, l_ref = refs
    here = here_ref[0]
    for n, ref in enumerate(near_refs):
        l_ref[here ^ (2 * n)] = ref[0]
        l_ref[here ^ (2 * n + 1)] = far_ref[n]
    parts, both, lanes = right_ref.shape
    rows = both // 2
    col_count = parts // row_count
    size = lanes // own
    outer = rows // size
    tiles = sum_ref.shape[1]
    for t in range(2):
        masks = channel_masks(sum_ref.at[t], own, lanes)

        def block_of(ref, block):
            r, h = block // outer, block % outer
            at = t * rows + h * size
            return [
                ref[r * col_count + c, at : at + size, :] for c in range(tiles)
            ]

        right = jnp.concatenate(
            [
                jnp.concatenate(block_of(right_ref, block), axis=1)
                for block in range(tiles)
            ],
            axis=0,
        )
        for r in range(row_count // 2):

            def put(h, piece):
                at = t * rows + h * size
                for c in range(col_count):
                    x_ref[r * col_count + c, at : at + size, :] = piece[
                        c * size : (c + 1) * size, :
                    ]

            blocks = range(r * outer, (r + 1) * outer)
            multiply(
                right,
                [block_of(l_ref, block) for block in blocks],
                masks,
                row_ref,
                [lane_ref[block : block + 1, :] for block in blocks],
                2 * here + t,
                size,
                put,
            )


def product1_kernel(
    row_count, own, here_ref, got_ref, sum_ref, lane_ref, row_ref, x_ref
):
    parts, both, lanes = got_ref.shape
    rows = both // 2
    col_count = parts // row_count
    size = lanes // own
    outer = rows // size
    tiles = lane_ref.shape[0]
    masks = channel_masks(sum_ref.at[2], own, lanes)

    def block_of(side, block):
        return [
            got_ref[
                t // outer * col_count + block,
                side * rows + t % outer * size : side * rows + (t % outer + 1) * size,
                :,
            ]
            for t in range(tiles)
        ]

    right = jnp.concatenate(
        [jnp.concatenate(block_of(1, block), axis=1) for block in range(tiles)], axis=0
    )
    for r in range(row_count):

        def put(h, piece):
            for c in range(col_count):
                x_ref[r * col_count + c, h * size : (h + 1) * size, :] = piece[
                    c * size : (c + 1) * size, :
                ]

        blocks = range(r * outer, (r + 1) * outer)
        multiply(
            right,
            [block_of(0, block) for block in blocks],
            masks,
            row_ref,
            [lane_ref[block : block + 1, :] for block in blocks],
            here_ref[1],
            size,
            put,
        )


def gather_lanes(x_ref, u_ref):
    size = x_ref.shape[0]
    cols = u_ref.shape[1]
    outer = u_ref.shape[0] // size
    for o in range(outer):
        for b in range(0, cols, PACK):
            at = o * cols + b
            got = pick_lanes(
                [x_ref[-d % size, at : at + PACK, :] for d in range(size)], 1, True
            )
            for v in range(size):
                u_ref[o * size + v, b : b + PACK, :] = turn_lanes(got[v], v, size)


def finish_rows(layer, at, step, u_ref, pair_ref, gate_ref, gain_ref, bias_ref, w_out):
    _, cols_n, width = pair_ref.shape
    flat = (step * cols_n, width)
    x = beside(u_ref[at : at + step].reshape(flat))
    y = norm_beside(x, gain_ref[layer, 1:2, :], bias_ref[layer, 1:2, :])
    update = below(jnp.dot(y, w_out, preferred_element_type=jnp.float32))
    base = pair_ref[at : at + step].astype(jnp.float32).reshape(flat)
    return (base + gate_ref[at : at + step].reshape(flat) * update).astype(jnp.bfloat16)


def middle_kernel(
    x_ref, pair_ref, gate_ref, w_out_ref, w_in_ref, gain_ref, bias_ref,
    mid_ref, send_ref, u_ref, l_ref, r_ref,
):
    rows_n, cols_n, width = pair_ref.shape
    size = send_ref.shape[0]
    gather_lanes(x_ref, u_ref)
    mid = finish_rows(
        0, 0, rows_n, u_ref, pair_ref, gate_ref, gain_ref, bias_ref, w_out_ref[...]
    )
    mid_ref[...] = mid.reshape(rows_n, cols_n, width)
    normed = norm_rows(mid, gain_ref[1, 0:1, :], bias_ref[1, 0:1, :])
    left, right = gated(normed, w_in_ref[...], width)
    put_rolled(l_ref, 0, left, cols_n, size)
    put_rolled(r_ref, 0, right, cols_n, size)
    for side, ref in enumerate((l_ref, r_ref)):

        def put(d, at, part, ahead=side * rows_n):
            send_ref[d, ahead + at : ahead + at + PACK, :] = part

        scatter_lanes(ref, size, put)


def close_kernel(
    x_ref, pair_ref, gate_ref, w_out_ref, gain_ref, bias_ref, out_ref, u_ref
):
    rows_n, cols_n, width = pair_ref.shape
    gather_lanes(x_ref, u_ref)
    step = CLOSE_STEP
    for i in range(0, rows_n, step):
        out = finish_rows(
            1, i, step, u_ref, pair_ref, gate_ref, gain_ref, bias_ref, w_out_ref[...]
        )
        out_ref[i : i + step] = out.reshape(step, cols_n, width)


VMEM = pl.BlockSpec(memory_space=pltpu.VMEM)
SMEM = pl.BlockSpec(memory_space=pltpu.SMEM)
HBM = pl.BlockSpec(memory_space=pltpu.HBM)


def call(body, name, specs, outs, scratch, flops, moved, grant=40 * 2**20):
    return pl.pallas_call(
        body,
        name=name,
        in_specs=specs,
        out_specs=jax.tree.map(lambda _: VMEM, outs),
        out_shape=outs,
        scratch_shapes=scratch,
        cost_estimate=pl.CostEstimate(flops=flops, bytes_accessed=moved, transcendentals=0),
        compiler_params=pltpu.CompilerParams(vmem_limit_bytes=grant),
    )


NEAR = ("sub", "col")
ALL = ("half", "sub", "col")


def fast(pair, residue_mask, norm_gain, norm_bias, w_in_q, exp_in, w_out_q, exp_out):
    rows_n, cols_n, width = pair.shape
    row_count, col_count = 2 * lax.axis_size("sub"), lax.axis_size("col")
    parts = row_count * col_count
    near = parts // 2
    own = width // parts
    tokens = residue_mask.shape[0]
    bf16, f32 = jnp.bfloat16, jnp.float32
    half = lax.axis_index("half")
    within = lax.axis_index("sub") * col_count + lax.axis_index("col")
    here = half * near + within
    numbers = jnp.stack([within, here])
    mask = residue_mask.astype(f32)
    by_col = mask.reshape(tokens // cols_n, cols_n)
    lane_mask = jnp.tile(by_col, (1, own))
    half_mask = lax.dynamic_slice_in_dim(
        lane_mask, half * (lane_mask.shape[0] // 2), lane_mask.shape[0] // 2
    )
    row_mask = jnp.broadcast_to(mask[:, None], (tokens, width))
    def sum_mask(group):
        return jnp.repeat(jnp.roll(by_col, group, axis=1), own, axis=1)

    block = (rows_n, cols_n, width)
    sent = jax.ShapeDtypeStruct((parts, 2 * rows_n, width), bf16)
    back0 = jax.ShapeDtypeStruct((near, 2 * rows_n, width), bf16)
    back1 = jax.ShapeDtypeStruct((parts, rows_n, width), bf16)
    pairs = rows_n * cols_n
    proj_cost = (2 * pairs * width * 4 * width, 8 * pairs * width)
    product_cost = (2 * tokens * tokens * tokens * own * own, 6 * pairs * width)
    side = pltpu.VMEM(block, bf16)
    gate_outs = (
        jax.ShapeDtypeStruct(block, f32),
        jax.ShapeDtypeStruct((2 * width, 2 * width), bf16),
        jax.ShapeDtypeStruct((width, 4 * width), bf16),
    )

    def gate(layer, source):
        return call(
            functools.partial(gate_kernel, layer, parts), f"gate{layer}",
            [VMEM, VMEM, VMEM, VMEM, SMEM, VMEM, SMEM], gate_outs[: 3 - layer], [],
            2 * pairs * width * width, 8 * pairs * width,
        )(source, norm_gain, norm_bias, w_in_q, exp_in, w_out_q, exp_out)

    def exchange(x, axes=ALL):
        return lax.all_to_all(x, axes, 0, 0, tiled=True)

    turned = pltpu.VMEM((cols_n, rows_n, width), bf16)
    flat = pltpu.VMEM((pairs, width), f32)
    send, gain0 = call(
        right_kernel, "right0", [HBM] * 5,
        (sent, jax.ShapeDtypeStruct(norm_gain.shape, f32)),
        [
            side,
            pltpu.VMEM(norm_gain.shape, f32),
            pltpu.VMEM(norm_bias.shape, f32),
            pltpu.VMEM((1, width, 2 * width), bf16),
            pltpu.SMEM(exp_in.shape, jnp.int32),
            flat,
            turned,
            pltpu.SemaphoreType.DMA((5,)),
        ],
        *proj_cost, grant=None,
    )(pair, norm_gain, norm_bias, w_in_q, exp_in)
    right = exchange(send)

    two = jax.ShapeDtypeStruct((2, 2 * rows_n, width), bf16)
    chips = near // 2
    lefts = call(
        left_kernel, "left0", [SMEM, VMEM, VMEM, VMEM, VMEM, SMEM], (two,) * chips,
        [flat, turned, pltpu.VMEM((near, 2 * rows_n, width), bf16)], *proj_cost,
    )(numbers, pair, gain0, norm_bias, w_in_q, exp_in)

    def across(x, offset):
        return lax.ppermute(x, NEAR, [(n, n ^ offset) for n in range(near)])

    lefts = [lefts[0]] + [across(lefts[n], 2 * n) for n in range(1, chips)]
    far = across(jnp.stack([left[1] for left in lefts]), 1)

    groups = (2 * within, 2 * within + 1, here)
    sum_masks = jnp.stack([sum_mask(group) for group in groups])
    x = call(
        functools.partial(product0_kernel, row_count, own), "product0",
        [SMEM] + [VMEM] * (5 + chips), back0,
        [pltpu.VMEM((near, 2 * rows_n, width), bf16)], *product_cost,
    )(
        numbers, right, sum_masks, half_mask, row_mask,
        *lefts, far,
    )
    x = exchange(x, NEAR).reshape(back1.shape)
    gate0, w_out, w_in = gate(0, pair)
    mid, send = call(
        middle_kernel, "middle", [VMEM] * 7,
        (jax.ShapeDtypeStruct(block, bf16), sent), [side, side, side], *proj_cost,
    )(x, pair, gate0, w_out, w_in, norm_gain, norm_bias)
    got = exchange(send)
    gate1, w_out = gate(1, mid)
    x = call(
        functools.partial(product1_kernel, row_count, own), "product1",
        [SMEM] + [VMEM] * 4, back1, [], *product_cost,
    )(numbers, got, sum_masks, lane_mask, row_mask)
    x = exchange(x)
    return call(
        close_kernel, "close", [VMEM] * 6,
        jax.ShapeDtypeStruct(block, bf16), [side], *proj_cost,
    )(x, mid, gate1, w_out, norm_gain, norm_bias)


def solution(mesh):
    row_count, col_count = mesh.shape["row"], mesh.shape["col"]
    parts = row_count * col_count

    def step(pair, *rest):
        width = pair.shape[2]
        rows_n, cols_n = pair.shape[0] // row_count, pair.shape[1] // col_count
        fits = (
            width == 128
            and width % parts == 0
            and parts & (parts - 1) == 0
            and row_count % 2 == 0
            and cols_n == parts
            and rows_n % cols_n == 0
            and cols_n % OPEN_STEP == 0
            and rows_n % CLOSE_STEP == 0
        )
        if fits:
            halves = jax.sharding.Mesh(
                mesh.devices.reshape(2, row_count // 2, col_count), ALL
            )
            body, over, placed = fast, halves, P(("half", "sub"), "col", None)
        else:
            body, over, placed = plain, mesh, P("row", "col", None)
        return jax.shard_map(
            body,
            mesh=over,
            in_specs=(placed,) + (P(),) * len(rest),
            out_specs=placed,
            check_vma=False,
        )(pair, *rest)

    return step
```

```python
import functools

import jax
import jax.numpy as jnp
from jax import lax
from jax.experimental import pallas as pl
from jax.experimental.pallas import tpu as pltpu
from jax.sharding import PartitionSpec as P

BLK = 32
AXES = ("row", "col")
EPS = 1e-05


def layer_norm(values, scale_vec, shift_vec):
    average = jnp.mean(values, axis=-1, keepdims=True)
    centred = values - average
    variance = jnp.mean(centred * centred, axis=-1, keepdims=True)
    return centred * lax.rsqrt(variance + EPS) * scale_vec + shift_vec


def dequantize(quantized, exponents, block_size):
    scales = jnp.exp2(exponents.astype(jnp.float32))
    scales = jnp.repeat(jnp.repeat(scales, block_size, axis=0), block_size, axis=1)
    return (quantized.astype(jnp.float32) * scales).astype(jnp.bfloat16)


def plain_update(layer, pair, row_mask, col_mask, norm_gain, norm_bias, w_in, w_out):
    rows_n, cols_n, width = pair.shape
    row_count, col_count = lax.axis_size("row"), lax.axis_size("col")
    parts = row_count * col_count
    own = width // parts
    normed = layer_norm(
        pair.astype(jnp.float32), norm_gain[layer, 0], norm_bias[layer, 0]
    ).astype(jnp.bfloat16)
    proj = jnp.einsum("ijc,cd->ijd", normed, w_in, preferred_element_type=jnp.float32)
    p0, p1, p2, p3, p4 = jnp.split(proj, 5, axis=-1)
    pm = (row_mask[:, None] * col_mask[None, :])[:, :, None]
    left = (jax.nn.sigmoid(p0) * p1 * pm).astype(jnp.bfloat16)
    right = (jax.nn.sigmoid(p2) * p3 * pm).astype(jnp.bfloat16)
    sent = jnp.stack([left, right]).reshape(2, rows_n, cols_n, parts, own)
    got = lax.all_to_all(sent.transpose(3, 0, 4, 1, 2), AXES, 0, 0, tiled=True)
    got = got.reshape(row_count, col_count, 2, own, rows_n, cols_n)
    whole = got.transpose(2, 3, 0, 4, 1, 5).reshape(
        2, own, row_count * rows_n, col_count * cols_n
    )
    spec = "cik,cjk->cij" if layer == 0 else "cki,ckj->cij"
    x = jnp.einsum(spec, whole[0], whole[1], preferred_element_type=jnp.float32)
    x = x.astype(jnp.bfloat16).reshape(own, row_count, rows_n, col_count, cols_n)
    back = x.transpose(1, 3, 0, 2, 4).reshape(parts, own, rows_n, cols_n)
    back = lax.all_to_all(back, AXES, 0, 0, tiled=True)
    x = back.transpose(2, 3, 0, 1).reshape(rows_n, cols_n, width)
    y = layer_norm(
        x.astype(jnp.float32), norm_gain[layer, 1], norm_bias[layer, 1]
    ).astype(jnp.bfloat16)
    out = jnp.einsum("ijc,cd->ijd", y, w_out, preferred_element_type=jnp.float32)
    return (pair.astype(jnp.float32) + jax.nn.sigmoid(p4) * out).astype(jnp.bfloat16)


def plain(pair, residue_mask, norm_gain, norm_bias, w_in_q, exp_in, w_out_q, exp_out):
    rows_n, cols_n, _ = pair.shape
    mask = residue_mask.astype(jnp.float32)
    row_mask = lax.dynamic_slice_in_dim(mask, lax.axis_index("row") * rows_n, rows_n)
    col_mask = lax.dynamic_slice_in_dim(mask, lax.axis_index("col") * cols_n, cols_n)
    for layer in range(2):
        w_in = dequantize(w_in_q[layer], exp_in[layer], BLK)
        w_out = dequantize(w_out_q[layer], exp_out[layer], BLK)
        pair = plain_update(
            layer, pair, row_mask, col_mask, norm_gain, norm_bias, w_in, w_out
        )
    return pair


PACK = 16


def pick_lanes(values, slot, back=False):
    size = len(values)
    lane = lax.broadcasted_iota(jnp.int32, values[0].shape, 1).astype(jnp.int16)
    step = 1
    while step < size:
        stay = (lane & jnp.int16(slot * step)) == 0
        move = -step if back else step
        values = [
            jnp.where(stay, values[v], values[(v + move) % size]) for v in range(size)
        ]
        step *= 2
    return values


def turn_lanes(value, by, size):
    if by == 0:
        return value
    lanes = value.shape[1]
    lane = lax.broadcasted_iota(jnp.int32, value.shape, 1).astype(jnp.int16)
    near = (lane & jnp.int16(size - 1)) < jnp.int16(size - by)
    return jnp.where(
        near, pltpu.roll(value, lanes - by, 1), pltpu.roll(value, size - by, 1)
    )


def twice(weights):
    none = jnp.zeros_like(weights)
    return jnp.concatenate(
        [
            jnp.concatenate([weights, none], axis=1),
            jnp.concatenate([none, weights], axis=1),
        ],
        axis=0,
    )


def beside(rows):
    half = rows.shape[0] // 2
    return jnp.concatenate([rows[:half], rows[half:]], axis=1)


def below(lanes):
    half = lanes.shape[1] // 2
    return jnp.concatenate([lanes[:, :half], lanes[:, half:]], axis=0)


def norm_beside(values, gain, bias):
    width = values.shape[1] // 2
    share = jnp.full((width, width), 1.0 / width, jnp.float32)
    row = lax.broadcasted_iota(jnp.int32, (width, width), 0)
    column = lax.broadcasted_iota(jnp.int32, (width, width), 1)
    centre = (row == column).astype(jnp.float32) - share
    centred = jnp.dot(
        values, twice(centre.astype(jnp.bfloat16)), preferred_element_type=jnp.float32
    )
    variance = jnp.dot(
        (centred * centred).astype(jnp.bfloat16),
        twice(share.astype(jnp.bfloat16)),
        preferred_element_type=jnp.float32,
    )
    gain = jnp.concatenate([gain, gain], axis=1)
    bias = jnp.concatenate([bias, bias], axis=1)
    return (centred * lax.rsqrt(variance + EPS) * gain + bias).astype(jnp.bfloat16)


def norm_rows(values, gain, bias):
    return below(norm_beside(beside(values), gain, bias))


def scaled(q_ref, exp_ref, layer, first, count, ahead=0):
    width = q_ref.shape[1]
    per = 128 // BLK
    block = lax.broadcasted_iota(jnp.int32, (1, 128), 1) // BLK
    tiles = []
    for t in range(first, first + count):
        rows = []
        for rb in range(width // BLK):
            e = jnp.zeros((1, 128), jnp.int32)
            for s in range(per):
                e = jnp.where(block == s, exp_ref[layer, rb, (ahead + t) * per + s], e)
            q = q_ref[layer, rb * BLK : (rb + 1) * BLK, t * 128 : (t + 1) * 128]
            scale = jnp.exp2(e.astype(jnp.float32))
            rows.append((q.astype(jnp.float32) * scale).astype(jnp.bfloat16))
        tiles.append(jnp.concatenate(rows, axis=0))
    return jnp.concatenate(tiles, axis=1)


def slotted(weights, width, size):
    slot = width // size
    row = lax.broadcasted_iota(jnp.int32, (width, width), 0)
    column = lax.broadcasted_iota(jnp.int32, (width, width), 1)
    order = (row == column % slot * size + column // slot).astype(jnp.bfloat16)
    tiles = [
        jnp.dot(
            weights[:, t : t + width], order, preferred_element_type=jnp.float32
        ).astype(jnp.bfloat16)
        for t in range(0, weights.shape[1], width)
    ]
    return jnp.concatenate(tiles, axis=1)


def gated(normed, weights, width):
    proj = jnp.dot(normed, weights, preferred_element_type=jnp.float32)
    return [
        jax.nn.sigmoid(proj[:, t : t + width]) * proj[:, t + width : t + 2 * width]
        for t in range(0, proj.shape[1], 2 * width)
    ]


def put_rolled(ref, at, values, rows, size):
    slot = values.shape[1] // size
    for s in range(values.shape[0] // rows):
        part = values[s * rows : (s + 1) * rows]
        shift = (at + s) % size * slot
        if shift:
            part = pltpu.roll(part, shift, 1)
        ref[at + s] = part.astype(jnp.bfloat16)


def scatter_lanes(ref, size, put):
    rows = ref.shape[1]
    for o in range(ref.shape[0] // size):
        for b in range(0, rows, PACK):
            got = pick_lanes(
                [ref[o * size + v, b : b + PACK, :] for v in range(size)],
                ref.shape[2] // size,
            )
            for d in range(size):
                put(d, o * rows + b, got[-d % size])


OPEN_STEP = 16


CLOSE_STEP = 32


def in_turn(count, first, second):
    ready = first(0)
    for n in range(count):
        following = first(n + 1) if n + 1 < count else None
        second(n, ready)
        ready = following


def own_number():
    return lax.axis_index("sub") * lax.axis_size("col") + lax.axis_index("col")


def operand(size, pair_ref, gain_ref, bias_ref, weights, t_ref, v_ref):
    rows_n, cols_n, width = pair_ref.shape
    gain, bias = gain_ref[0, 0:1, :], bias_ref[0, 0:1, :]
    t_ref[...] = pair_ref[...].astype(jnp.float32).reshape(t_ref.shape)
    step = OPEN_STEP

    def norm(n):
        part = jnp.concatenate(
            [
                t_ref[pl.ds(n * step + s, rows_n, stride=cols_n), :]
                for s in range(step)
            ],
            axis=0,
        )
        return norm_rows(part.astype(jnp.bfloat16), gain, bias)

    def project(n, normed):
        (made,) = gated(normed, weights, width)
        put_rolled(v_ref, n * step, made, rows_n, size)

    in_turn(cols_n // step, norm, project)


def right_kernel(
    pair_hbm, gain_hbm, bias_hbm, q_hbm, exp_hbm, send_ref, gain0_ref,
    pair_ref, gain_ref, bias_ref, q_ref, exp_ref, t_ref, v_ref, sems,
):
    first = q_ref.shape[2]
    moves = [
        pltpu.make_async_copy(source, target, sems.at[n])
        for n, (source, target) in enumerate(
            (
                (exp_hbm, exp_ref),
                (q_hbm.at[0:1, :, first : 2 * first], q_ref),
                (gain_hbm, gain_ref),
                (bias_hbm, bias_ref),
                (pair_hbm, pair_ref),
            )
        )
    ]
    for move in moves:
        move.start()
    for move in moves[:-1]:
        move.wait()
    width = pair_ref.shape[2]
    size = send_ref.shape[0]
    near = size // 2
    weights = slotted(scaled(q_ref, exp_ref, 0, 0, 2, 2), width, size)
    moves[-1].wait()
    gain0_ref[...] = gain_ref[...]
    operand(size, pair_ref, gain_ref, bias_ref, weights, t_ref, v_ref)
    rows = v_ref.shape[1]

    def put(d, at, part):
        at = d % 2 * rows + at
        send_ref[d // 2, at : at + PACK, :] = part
        send_ref[near + d // 2, at : at + PACK, :] = part

    scatter_lanes(v_ref, size, put)


def chip_order(chips):
    return [0, *range(chips // 2, chips), *range(1, chips // 2)]


def left_kernel(pair_ref, gain_ref, bias_ref, q_ref, exp_ref, *refs):
    own_ref, other_ref, t_ref, v_ref, o_ref = refs
    width = pair_ref.shape[2]
    size = 2 * o_ref.shape[0]
    weights = slotted(scaled(q_ref, exp_ref, 0, 0, 2), width, size)
    operand(size, pair_ref, gain_ref, bias_ref, weights, t_ref, v_ref)
    rows = v_ref.shape[1]
    here = own_number()

    def put(d, at, part):
        at = d % 2 * rows + at
        o_ref[here ^ (d // 2), at : at + PACK, :] = part

    scatter_lanes(v_ref, size, put)
    for n, m in enumerate(chip_order(own_ref.shape[0])):
        own_ref[n] = o_ref[2 * m]
        other_ref[n] = o_ref[2 * m + 1]


def pack_kernel(own_ref, other_ref, *outs):
    for n, out in enumerate(outs):
        out[0] = own_ref[n]
        out[1] = other_ref[n]


def gate_kernel(
    layer, size, pair_ref, gain_ref, bias_ref, q_ref, exp_ref, o_ref, oexp_ref,
    gate_ref, out_ref, *next_ref,
):
    rows_n, cols_n, width = pair_ref.shape
    weights = twice(scaled(q_ref, exp_ref, layer, 4, 1))
    gain, bias = gain_ref[layer, 0:1, :], bias_ref[layer, 0:1, :]
    out_ref[...] = twice(scaled(o_ref, oexp_ref, layer, 0, 1))
    if next_ref:
        next_ref[0][...] = slotted(scaled(q_ref, exp_ref, layer + 1, 0, 4), width, size)
    step = 16
    for i in range(0, rows_n, step):
        part = beside(pair_ref[i : i + step].reshape(step * cols_n, width))
        proj = jnp.dot(
            norm_beside(part, gain, bias), weights, preferred_element_type=jnp.float32
        )
        gate_ref[i : i + step] = below(jax.nn.sigmoid(proj)).reshape(step, cols_n, width)


def channel_masks(sum_ref, own, lanes):
    channel = lax.broadcasted_iota(jnp.int32, (1, lanes), 1) % own
    return [
        [
            jnp.where(channel == a, sum_ref[t : t + 1, :], 0.0).astype(jnp.bfloat16)
            for t in range(sum_ref.shape[0])
        ]
        for a in range(own)
    ]


def multiply(right, blocks, masks, row_ref, lane_rows, group, size, put):
    lanes = blocks[0][0].shape[1]
    lane = lax.broadcasted_iota(jnp.int32, (1, lanes), 1)
    turn = (lane & -size) + ((lane - group) & (size - 1))
    turn = jnp.broadcast_to(turn, (right.shape[0], lanes))
    left = jnp.concatenate(
        [
            jnp.concatenate([part * mask for part, mask in zip(parts, row)], axis=1)
            for parts in blocks
            for row in masks
        ],
        axis=0,
    )
    x = lax.dot_general(
        right, left, (((1,), (1,)), ((), ())), preferred_element_type=jnp.float32
    )
    for h in range(len(blocks)):
        piece = x[:, h * lanes : (h + 1) * lanes] * row_ref[...] * lane_rows[h]
        piece = jnp.take_along_axis(piece, turn, axis=1, mode="promise_in_bounds")
        put(h, piece.astype(jnp.bfloat16))


def product0_kernel(
    row_count, own, right_ref, sum_ref, lane_ref, row_ref, *refs
):
    *left_refs, x_ref, l_ref = refs
    here = own_number()
    for ref, m in zip(left_refs, chip_order(len(left_refs))):
        l_ref[here ^ (2 * m)] = ref[0]
        l_ref[here ^ (2 * m + 1)] = ref[1]
    parts, both, lanes = right_ref.shape
    rows = both // 2
    col_count = parts // row_count
    size = lanes // own
    outer = rows // size
    tiles = sum_ref.shape[1]
    for t in range(2):
        masks = channel_masks(sum_ref.at[t], own, lanes)

        def block_of(ref, block):
            r, h = block // outer, block % outer
            at = t * rows + h * size
            return [
                ref[r * col_count + c, at : at + size, :] for c in range(tiles)
            ]

        right = jnp.concatenate(
            [
                jnp.concatenate(block_of(right_ref, block), axis=1)
                for block in range(tiles)
            ],
            axis=0,
        )
        for r in range(row_count // 2):

            def put(h, piece):
                at = t * rows + h * size
                for c in range(col_count):
                    x_ref[r * col_count + c, at : at + size, :] = piece[
                        c * size : (c + 1) * size, :
                    ]

            blocks = range(r * outer, (r + 1) * outer)
            multiply(
                right,
                [block_of(l_ref, block) for block in blocks],
                masks,
                row_ref,
                [lane_ref[block : block + 1, :] for block in blocks],
                2 * here + t,
                size,
                put,
            )


def product1_kernel(
    row_count, own, got_ref, sum_ref, lane_ref, row_ref, x_ref
):
    parts, both, lanes = got_ref.shape
    rows = both // 2
    col_count = parts // row_count
    size = lanes // own
    outer = rows // size
    tiles = lane_ref.shape[0]
    masks = channel_masks(sum_ref.at[2], own, lanes)

    def block_of(side, block):
        return [
            got_ref[
                t // outer * col_count + block,
                side * rows + t % outer * size : side * rows + (t % outer + 1) * size,
                :,
            ]
            for t in range(tiles)
        ]

    right = jnp.concatenate(
        [jnp.concatenate(block_of(1, block), axis=1) for block in range(tiles)], axis=0
    )
    for r in range(row_count):

        def put(h, piece):
            for c in range(col_count):
                x_ref[r * col_count + c, h * size : (h + 1) * size, :] = piece[
                    c * size : (c + 1) * size, :
                ]

        blocks = range(r * outer, (r + 1) * outer)
        multiply(
            right,
            [block_of(0, block) for block in blocks],
            masks,
            row_ref,
            [lane_ref[block : block + 1, :] for block in blocks],
            lax.axis_index("half") * (parts // 2) + own_number(),
            size,
            put,
        )


def gather_lanes(x_ref, u_ref):
    size = x_ref.shape[0]
    cols = u_ref.shape[1]
    outer = u_ref.shape[0] // size
    for o in range(outer):
        for b in range(0, cols, PACK):
            at = o * cols + b
            got = pick_lanes(
                [x_ref[-d % size, at : at + PACK, :] for d in range(size)], 1, True
            )
            for v in range(size):
                u_ref[o * size + v, b : b + PACK, :] = turn_lanes(got[v], v, size)


def finish_rows(layer, at, step, u_ref, pair_ref, gate_ref, gain_ref, bias_ref, w_out):
    _, cols_n, width = pair_ref.shape
    flat = (step * cols_n, width)
    x = beside(u_ref[at : at + step].reshape(flat))
    y = norm_beside(x, gain_ref[layer, 1:2, :], bias_ref[layer, 1:2, :])
    update = below(jnp.dot(y, w_out, preferred_element_type=jnp.float32))
    base = pair_ref[at : at + step].astype(jnp.float32).reshape(flat)
    return (base + gate_ref[at : at + step].reshape(flat) * update).astype(jnp.bfloat16)


def middle_kernel(
    x_ref, pair_ref, gate_ref, w_out_ref, w_in_ref, gain_ref, bias_ref,
    mid_ref, send_ref, u_ref, l_ref, r_ref,
):
    rows_n, cols_n, width = pair_ref.shape
    size = send_ref.shape[0]
    gather_lanes(x_ref, u_ref)
    mid = finish_rows(
        0, 0, rows_n, u_ref, pair_ref, gate_ref, gain_ref, bias_ref, w_out_ref[...]
    )
    mid_ref[...] = mid.reshape(rows_n, cols_n, width)
    normed = norm_rows(mid, gain_ref[1, 0:1, :], bias_ref[1, 0:1, :])
    left, right = gated(normed, w_in_ref[...], width)
    put_rolled(l_ref, 0, left, cols_n, size)
    put_rolled(r_ref, 0, right, cols_n, size)
    for side, ref in enumerate((l_ref, r_ref)):

        def put(d, at, part, ahead=side * rows_n):
            send_ref[d, ahead + at : ahead + at + PACK, :] = part

        scatter_lanes(ref, size, put)


def close_kernel(
    x_ref, pair_ref, gate_ref, w_out_ref, gain_ref, bias_ref, out_ref, u_ref
):
    rows_n, cols_n, width = pair_ref.shape
    gather_lanes(x_ref, u_ref)
    step = CLOSE_STEP
    for i in range(0, rows_n, step):
        out = finish_rows(
            1, i, step, u_ref, pair_ref, gate_ref, gain_ref, bias_ref, w_out_ref[...]
        )
        out_ref[i : i + step] = out.reshape(step, cols_n, width)


VMEM = pl.BlockSpec(memory_space=pltpu.VMEM)
SMEM = pl.BlockSpec(memory_space=pltpu.SMEM)
HBM = pl.BlockSpec(memory_space=pltpu.HBM)


def call(body, name, specs, outs, scratch, flops, moved, grant=40 * 2**20):
    return pl.pallas_call(
        body,
        name=name,
        in_specs=specs,
        out_specs=jax.tree.map(lambda _: VMEM, outs),
        out_shape=outs,
        scratch_shapes=scratch,
        cost_estimate=pl.CostEstimate(flops=flops, bytes_accessed=moved, transcendentals=0),
        compiler_params=pltpu.CompilerParams(vmem_limit_bytes=grant),
    )


NEAR = ("sub", "col")
ALL = ("half", "sub", "col")


def fast(pair, residue_mask, norm_gain, norm_bias, w_in_q, exp_in, w_out_q, exp_out):
    rows_n, cols_n, width = pair.shape
    row_count, col_count = 2 * lax.axis_size("sub"), lax.axis_size("col")
    parts = row_count * col_count
    near = parts // 2
    own = width // parts
    tokens = residue_mask.shape[0]
    bf16, f32 = jnp.bfloat16, jnp.float32
    half = lax.axis_index("half")
    within = lax.axis_index("sub") * col_count + lax.axis_index("col")
    here = half * near + within
    mask = residue_mask.astype(f32)
    by_col = mask.reshape(tokens // cols_n, cols_n)
    lane_mask = jnp.tile(by_col, (1, own))
    half_mask = lax.dynamic_slice_in_dim(
        lane_mask, half * (lane_mask.shape[0] // 2), lane_mask.shape[0] // 2
    )
    row_mask = jnp.broadcast_to(mask[:, None], (tokens, width))
    def sum_mask(group):
        return jnp.repeat(jnp.roll(by_col, group, axis=1), own, axis=1)

    block = (rows_n, cols_n, width)
    sent = jax.ShapeDtypeStruct((parts, 2 * rows_n, width), bf16)
    back0 = jax.ShapeDtypeStruct((near, 2 * rows_n, width), bf16)
    back1 = jax.ShapeDtypeStruct((parts, rows_n, width), bf16)
    pairs = rows_n * cols_n
    proj_cost = (2 * pairs * width * 4 * width, 8 * pairs * width)
    product_cost = (2 * tokens * tokens * tokens * own * own, 6 * pairs * width)
    side = pltpu.VMEM(block, bf16)
    gate_outs = (
        jax.ShapeDtypeStruct(block, f32),
        jax.ShapeDtypeStruct((2 * width, 2 * width), bf16),
        jax.ShapeDtypeStruct((width, 4 * width), bf16),
    )

    def gate(layer, source):
        return call(
            functools.partial(gate_kernel, layer, parts), f"gate{layer}",
            [VMEM, VMEM, VMEM, VMEM, SMEM, VMEM, SMEM], gate_outs[: 3 - layer], [],
            2 * pairs * width * width, 8 * pairs * width,
        )(source, norm_gain, norm_bias, w_in_q, exp_in, w_out_q, exp_out)

    def exchange(x, axes=ALL):
        return lax.all_to_all(x, axes, 0, 0, tiled=True)

    turned = pltpu.VMEM((cols_n, rows_n, width), bf16)
    flat = pltpu.VMEM((pairs, width), f32)
    send, gain0 = call(
        right_kernel, "right0", [HBM] * 5,
        (sent, jax.ShapeDtypeStruct(norm_gain.shape, f32)),
        [
            side,
            pltpu.VMEM(norm_gain.shape, f32),
            pltpu.VMEM(norm_bias.shape, f32),
            pltpu.VMEM((1, width, 2 * width), bf16),
            pltpu.SMEM(exp_in.shape, jnp.int32),
            flat,
            turned,
            pltpu.SemaphoreType.DMA((5,)),
        ],
        *proj_cost, grant=None,
    )(pair, norm_gain, norm_bias, w_in_q, exp_in)
    right = exchange(send)

    chips = near // 2
    two = jax.ShapeDtypeStruct((2, 2 * rows_n, width), bf16)
    each = jax.ShapeDtypeStruct((chips, 2 * rows_n, width), bf16)
    mine, others = call(
        left_kernel, "left0", [VMEM, VMEM, VMEM, VMEM, SMEM], (each, each),
        [flat, turned, pltpu.VMEM((near, 2 * rows_n, width), bf16)], *proj_cost,
    )(pair, gain0, norm_bias, w_in_q, exp_in)

    def across(x, offset):
        return lax.ppermute(x, NEAR, [(n, n ^ offset) for n in range(near)])

    lefts = call(
        pack_kernel, "pack0", [VMEM, VMEM], (two,) * chips, [], 0, 4 * pairs * width
    )(mine, across(others, 1))
    lefts = [across(x, 2 * m) if m else x for x, m in zip(lefts, chip_order(chips))]

    groups = (2 * within, 2 * within + 1, here)
    sum_masks = jnp.stack([sum_mask(group) for group in groups])
    x = call(
        functools.partial(product0_kernel, row_count, own), "product0",
        [VMEM] * (4 + chips), back0,
        [pltpu.VMEM((near, 2 * rows_n, width), bf16)], *product_cost,
    )(
        right, sum_masks, half_mask, row_mask, *lefts,
    )
    x = exchange(x, NEAR).reshape(back1.shape)
    gate0, w_out, w_in = gate(0, pair)
    mid, send = call(
        middle_kernel, "middle", [VMEM] * 7,
        (jax.ShapeDtypeStruct(block, bf16), sent), [side, side, side], *proj_cost,
    )(x, pair, gate0, w_out, w_in, norm_gain, norm_bias)
    got = exchange(send)
    gate1, w_out = gate(1, mid)
    x = call(
        functools.partial(product1_kernel, row_count, own), "product1",
        [VMEM] * 4, back1, [], *product_cost,
    )(got, sum_masks, lane_mask, row_mask)
    x = exchange(x)
    return call(
        close_kernel, "close", [VMEM] * 6,
        jax.ShapeDtypeStruct(block, bf16), [side], *proj_cost,
    )(x, mid, gate1, w_out, norm_gain, norm_bias)


def solution(mesh):
    row_count, col_count = mesh.shape["row"], mesh.shape["col"]
    parts = row_count * col_count

    def step(pair, *rest):
        width = pair.shape[2]
        rows_n, cols_n = pair.shape[0] // row_count, pair.shape[1] // col_count
        fits = (
            width == 128
            and width % parts == 0
            and parts & (parts - 1) == 0
            and row_count % 2 == 0
            and cols_n == parts
            and rows_n % cols_n == 0
            and cols_n % OPEN_STEP == 0
            and rows_n % CLOSE_STEP == 0
        )
        if fits:
            halves = jax.sharding.Mesh(
                mesh.devices.reshape(2, row_count // 2, col_count), ALL
            )
            body, over, placed = fast, halves, P(("half", "sub"), "col", None)
        else:
            body, over, placed = plain, mesh, P("row", "col", None)
        return jax.shard_map(
            body,
            mesh=over,
            in_specs=(placed,) + (P(),) * len(rest),
            out_specs=placed,
            check_vma=False,
        )(pair, *rest)

    return step
```

```python
import functools

import jax
import jax.numpy as jnp
from jax import lax
from jax.experimental import pallas as pl
from jax.experimental.pallas import tpu as pltpu
from jax.sharding import PartitionSpec as P

BLK = 32
AXES = ("row", "col")
EPS = 1e-05


def layer_norm(values, scale_vec, shift_vec):
    average = jnp.mean(values, axis=-1, keepdims=True)
    centred = values - average
    variance = jnp.mean(centred * centred, axis=-1, keepdims=True)
    return centred * lax.rsqrt(variance + EPS) * scale_vec + shift_vec


def dequantize(quantized, exponents, block_size):
    scales = jnp.exp2(exponents.astype(jnp.float32))
    scales = jnp.repeat(jnp.repeat(scales, block_size, axis=0), block_size, axis=1)
    return (quantized.astype(jnp.float32) * scales).astype(jnp.bfloat16)


def plain_update(layer, pair, row_mask, col_mask, norm_gain, norm_bias, w_in, w_out):
    rows_n, cols_n, width = pair.shape
    row_count, col_count = lax.axis_size("row"), lax.axis_size("col")
    parts = row_count * col_count
    own = width // parts
    normed = layer_norm(
        pair.astype(jnp.float32), norm_gain[layer, 0], norm_bias[layer, 0]
    ).astype(jnp.bfloat16)
    proj = jnp.einsum("ijc,cd->ijd", normed, w_in, preferred_element_type=jnp.float32)
    p0, p1, p2, p3, p4 = jnp.split(proj, 5, axis=-1)
    pm = (row_mask[:, None] * col_mask[None, :])[:, :, None]
    left = (jax.nn.sigmoid(p0) * p1 * pm).astype(jnp.bfloat16)
    right = (jax.nn.sigmoid(p2) * p3 * pm).astype(jnp.bfloat16)
    sent = jnp.stack([left, right]).reshape(2, rows_n, cols_n, parts, own)
    got = lax.all_to_all(sent.transpose(3, 0, 4, 1, 2), AXES, 0, 0, tiled=True)
    got = got.reshape(row_count, col_count, 2, own, rows_n, cols_n)
    whole = got.transpose(2, 3, 0, 4, 1, 5).reshape(
        2, own, row_count * rows_n, col_count * cols_n
    )
    spec = "cik,cjk->cij" if layer == 0 else "cki,ckj->cij"
    x = jnp.einsum(spec, whole[0], whole[1], preferred_element_type=jnp.float32)
    x = x.astype(jnp.bfloat16).reshape(own, row_count, rows_n, col_count, cols_n)
    back = x.transpose(1, 3, 0, 2, 4).reshape(parts, own, rows_n, cols_n)
    back = lax.all_to_all(back, AXES, 0, 0, tiled=True)
    x = back.transpose(2, 3, 0, 1).reshape(rows_n, cols_n, width)
    y = layer_norm(
        x.astype(jnp.float32), norm_gain[layer, 1], norm_bias[layer, 1]
    ).astype(jnp.bfloat16)
    out = jnp.einsum("ijc,cd->ijd", y, w_out, preferred_element_type=jnp.float32)
    return (pair.astype(jnp.float32) + jax.nn.sigmoid(p4) * out).astype(jnp.bfloat16)


def plain(pair, residue_mask, norm_gain, norm_bias, w_in_q, exp_in, w_out_q, exp_out):
    rows_n, cols_n, _ = pair.shape
    mask = residue_mask.astype(jnp.float32)
    row_mask = lax.dynamic_slice_in_dim(mask, lax.axis_index("row") * rows_n, rows_n)
    col_mask = lax.dynamic_slice_in_dim(mask, lax.axis_index("col") * cols_n, cols_n)
    for layer in range(2):
        w_in = dequantize(w_in_q[layer], exp_in[layer], BLK)
        w_out = dequantize(w_out_q[layer], exp_out[layer], BLK)
        pair = plain_update(
            layer, pair, row_mask, col_mask, norm_gain, norm_bias, w_in, w_out
        )
    return pair


PACK = 16


def pick_lanes(values, slot, back=False):
    size = len(values)
    lane = lax.broadcasted_iota(jnp.int32, values[0].shape, 1).astype(jnp.int16)
    step = 1
    while step < size:
        stay = (lane & jnp.int16(slot * step)) == 0
        move = -step if back else step
        values = [
            jnp.where(stay, values[v], values[(v + move) % size]) for v in range(size)
        ]
        step *= 2
    return values


def turn_lanes(value, by, size):
    if by == 0:
        return value
    lanes = value.shape[1]
    lane = lax.broadcasted_iota(jnp.int32, value.shape, 1).astype(jnp.int16)
    near = (lane & jnp.int16(size - 1)) < jnp.int16(size - by)
    return jnp.where(
        near, pltpu.roll(value, lanes - by, 1), pltpu.roll(value, size - by, 1)
    )


def twice(weights):
    none = jnp.zeros_like(weights)
    return jnp.concatenate(
        [
            jnp.concatenate([weights, none], axis=1),
            jnp.concatenate([none, weights], axis=1),
        ],
        axis=0,
    )


def beside(rows):
    half = rows.shape[0] // 2
    return jnp.concatenate([rows[:half], rows[half:]], axis=1)


def below(lanes):
    half = lanes.shape[1] // 2
    return jnp.concatenate([lanes[:, :half], lanes[:, half:]], axis=0)


def norm_beside(values, gain, bias):
    width = values.shape[1] // 2
    share = jnp.full((width, width), 1.0 / width, jnp.float32)
    row = lax.broadcasted_iota(jnp.int32, (width, width), 0)
    column = lax.broadcasted_iota(jnp.int32, (width, width), 1)
    centre = (row == column).astype(jnp.float32) - share
    centred = jnp.dot(
        values, twice(centre.astype(jnp.bfloat16)), preferred_element_type=jnp.float32
    )
    variance = jnp.dot(
        (centred * centred).astype(jnp.bfloat16),
        twice(share.astype(jnp.bfloat16)),
        preferred_element_type=jnp.float32,
    )
    gain = jnp.concatenate([gain, gain], axis=1)
    bias = jnp.concatenate([bias, bias], axis=1)
    return (centred * lax.rsqrt(variance + EPS) * gain + bias).astype(jnp.bfloat16)


def norm_rows(values, gain, bias):
    return below(norm_beside(beside(values), gain, bias))


def scaled(q_ref, exp_ref, layer, first, count, ahead=0):
    width = q_ref.shape[1]
    per = 128 // BLK
    block = lax.broadcasted_iota(jnp.int32, (1, 128), 1) // BLK
    tiles = []
    for t in range(first, first + count):
        rows = []
        for rb in range(width // BLK):
            e = jnp.zeros((1, 128), jnp.int32)
            for s in range(per):
                e = jnp.where(block == s, exp_ref[layer, rb, (ahead + t) * per + s], e)
            q = q_ref[layer, rb * BLK : (rb + 1) * BLK, t * 128 : (t + 1) * 128]
            scale = jnp.exp2(e.astype(jnp.float32))
            rows.append((q.astype(jnp.float32) * scale).astype(jnp.bfloat16))
        tiles.append(jnp.concatenate(rows, axis=0))
    return jnp.concatenate(tiles, axis=1)


def slotted(weights, width, size):
    slot = width // size
    row = lax.broadcasted_iota(jnp.int32, (width, width), 0)
    column = lax.broadcasted_iota(jnp.int32, (width, width), 1)
    order = (row == column % slot * size + column // slot).astype(jnp.bfloat16)
    tiles = [
        jnp.dot(
            weights[:, t : t + width], order, preferred_element_type=jnp.float32
        ).astype(jnp.bfloat16)
        for t in range(0, weights.shape[1], width)
    ]
    return jnp.concatenate(tiles, axis=1)


def gated(normed, weights, width):
    proj = jnp.dot(normed, weights, preferred_element_type=jnp.float32)
    return [
        jax.nn.sigmoid(proj[:, t : t + width]) * proj[:, t + width : t + 2 * width]
        for t in range(0, proj.shape[1], 2 * width)
    ]


def put_rolled(ref, at, values, rows, size):
    slot = values.shape[1] // size
    for s in range(values.shape[0] // rows):
        part = values[s * rows : (s + 1) * rows]
        shift = (at + s) % size * slot
        if shift:
            part = pltpu.roll(part, shift, 1)
        ref[at + s] = part.astype(jnp.bfloat16)


def scatter_lanes(ref, size, put):
    rows = ref.shape[1]
    for o in range(ref.shape[0] // size):
        for b in range(0, rows, PACK):
            got = pick_lanes(
                [ref[o * size + v, b : b + PACK, :] for v in range(size)],
                ref.shape[2] // size,
            )
            for d in range(size):
                put(d, o * rows + b, got[-d % size])


OPEN_STEP = 16


CLOSE_STEP = 32


def in_turn(count, first, second):
    ready = first(0)
    for n in range(count):
        following = first(n + 1) if n + 1 < count else None
        second(n, ready)
        ready = following


def own_number():
    return lax.axis_index("sub") * lax.axis_size("col") + lax.axis_index("col")


def operand(size, pair_ref, gain_ref, bias_ref, weights, t_ref, v_ref):
    rows_n, cols_n, width = pair_ref.shape
    gain, bias = gain_ref[0, 0:1, :], bias_ref[0, 0:1, :]
    t_ref[...] = pair_ref[...].astype(jnp.float32).reshape(t_ref.shape)
    step = OPEN_STEP

    def norm(n):
        part = jnp.concatenate(
            [
                t_ref[pl.ds(n * step + s, rows_n, stride=cols_n), :]
                for s in range(step)
            ],
            axis=0,
        )
        return norm_rows(part.astype(jnp.bfloat16), gain, bias)

    def project(n, normed):
        (made,) = gated(normed, weights, width)
        put_rolled(v_ref, n * step, made, rows_n, size)

    in_turn(cols_n // step, norm, project)


def right_kernel(
    pair_hbm, gain_hbm, bias_hbm, q_hbm, exp_hbm, send_ref, gain0_ref,
    pair_ref, gain_ref, bias_ref, q_ref, exp_ref, t_ref, v_ref, sems,
):
    first = q_ref.shape[2]
    moves = [
        pltpu.make_async_copy(source, target, sems.at[n])
        for n, (source, target) in enumerate(
            (
                (exp_hbm, exp_ref),
                (q_hbm.at[0:1, :, first : 2 * first], q_ref),
                (gain_hbm, gain_ref),
                (bias_hbm, bias_ref),
                (pair_hbm, pair_ref),
            )
        )
    ]
    for move in moves:
        move.start()
    for move in moves[:-1]:
        move.wait()
    width = pair_ref.shape[2]
    size = send_ref.shape[0]
    near = size // 2
    weights = slotted(scaled(q_ref, exp_ref, 0, 0, 2, 2), width, size)
    moves[-1].wait()
    gain0_ref[...] = gain_ref[...]
    operand(size, pair_ref, gain_ref, bias_ref, weights, t_ref, v_ref)
    rows = v_ref.shape[1]

    def put(d, at, part):
        at = d % 2 * rows + at
        send_ref[d // 2, at : at + PACK, :] = part
        send_ref[near + d // 2, at : at + PACK, :] = part

    scatter_lanes(v_ref, size, put)


def chip_order(chips):
    return [0, *range(chips // 2, chips), *range(1, chips // 2)]


def left_kernel(pair_ref, gain_ref, bias_ref, q_ref, exp_ref, *refs):
    own_ref, other_ref, t_ref, v_ref, o_ref = refs
    width = pair_ref.shape[2]
    size = 2 * o_ref.shape[0]
    weights = slotted(scaled(q_ref, exp_ref, 0, 0, 2), width, size)
    operand(size, pair_ref, gain_ref, bias_ref, weights, t_ref, v_ref)
    rows = v_ref.shape[1]
    here = own_number()

    def put(d, at, part):
        at = d % 2 * rows + at
        o_ref[here ^ (d // 2), at : at + PACK, :] = part

    scatter_lanes(v_ref, size, put)
    for n, m in enumerate(chip_order(own_ref.shape[0])):
        own_ref[n] = o_ref[2 * m]
        other_ref[n] = o_ref[2 * m + 1]


def pack_kernel(own_ref, other_ref, *outs):
    for n, out in enumerate(outs):
        out[0] = own_ref[n]
        out[1] = other_ref[n]


def weights_kernel(size, _, q_ref, exp_ref, o_ref, oexp_ref, in_ref, gate_ref, out_ref):
    width = q_ref.shape[1]
    in_ref[...] = slotted(scaled(q_ref, exp_ref, 1, 0, 4), width, size)
    for layer in range(2):
        gate_ref[layer] = twice(scaled(q_ref, exp_ref, layer, 4, 1))
        out_ref[layer] = twice(scaled(o_ref, oexp_ref, layer, 0, 1))


def channel_masks(sum_ref, own, lanes):
    channel = lax.broadcasted_iota(jnp.int32, (1, lanes), 1) % own
    return [
        [
            jnp.where(channel == a, sum_ref[t : t + 1, :], 0.0).astype(jnp.bfloat16)
            for t in range(sum_ref.shape[0])
        ]
        for a in range(own)
    ]


def multiply(right, blocks, masks, row_ref, lane_rows, group, size, put):
    lanes = blocks[0][0].shape[1]
    lane = lax.broadcasted_iota(jnp.int32, (1, lanes), 1)
    turn = (lane & -size) + ((lane - group) & (size - 1))
    turn = jnp.broadcast_to(turn, (right.shape[0], lanes))
    left = jnp.concatenate(
        [
            jnp.concatenate([part * mask for part, mask in zip(parts, row)], axis=1)
            for parts in blocks
            for row in masks
        ],
        axis=0,
    )
    x = lax.dot_general(
        right, left, (((1,), (1,)), ((), ())), preferred_element_type=jnp.float32
    )
    for h in range(len(blocks)):
        piece = x[:, h * lanes : (h + 1) * lanes] * row_ref[...] * lane_rows[h]
        piece = jnp.take_along_axis(piece, turn, axis=1, mode="promise_in_bounds")
        put(h, piece.astype(jnp.bfloat16))


def product0_kernel(
    row_count, own, _, right_ref, sum_ref, lane_ref, row_ref, *refs
):
    *left_refs, x_ref, l_ref = refs
    here = own_number()
    for ref, m in zip(left_refs, chip_order(len(left_refs))):
        l_ref[here ^ (2 * m)] = ref[0]
        l_ref[here ^ (2 * m + 1)] = ref[1]
    parts, both, lanes = right_ref.shape
    rows = both // 2
    col_count = parts // row_count
    size = lanes // own
    outer = rows // size
    tiles = sum_ref.shape[1]
    for t in range(2):
        masks = channel_masks(sum_ref.at[t], own, lanes)

        def block_of(ref, block):
            r, h = block // outer, block % outer
            at = t * rows + h * size
            return [
                ref[r * col_count + c, at : at + size, :] for c in range(tiles)
            ]

        right = jnp.concatenate(
            [
                jnp.concatenate(block_of(right_ref, block), axis=1)
                for block in range(tiles)
            ],
            axis=0,
        )
        for r in range(row_count // 2):

            def put(h, piece):
                at = t * rows + h * size
                for c in range(col_count):
                    x_ref[r * col_count + c, at : at + size, :] = piece[
                        c * size : (c + 1) * size, :
                    ]

            blocks = range(r * outer, (r + 1) * outer)
            multiply(
                right,
                [block_of(l_ref, block) for block in blocks],
                masks,
                row_ref,
                [lane_ref[block : block + 1, :] for block in blocks],
                2 * here + t,
                size,
                put,
            )


def product1_kernel(
    row_count, own, got_ref, sum_ref, lane_ref, row_ref, x_ref
):
    parts, both, lanes = got_ref.shape
    rows = both // 2
    col_count = parts // row_count
    size = lanes // own
    outer = rows // size
    tiles = lane_ref.shape[0]
    masks = channel_masks(sum_ref.at[2], own, lanes)

    def block_of(side, block):
        return [
            got_ref[
                t // outer * col_count + block,
                side * rows + t % outer * size : side * rows + (t % outer + 1) * size,
                :,
            ]
            for t in range(tiles)
        ]

    right = jnp.concatenate(
        [jnp.concatenate(block_of(1, block), axis=1) for block in range(tiles)], axis=0
    )
    for r in range(row_count):

        def put(h, piece):
            for c in range(col_count):
                x_ref[r * col_count + c, h * size : (h + 1) * size, :] = piece[
                    c * size : (c + 1) * size, :
                ]

        blocks = range(r * outer, (r + 1) * outer)
        multiply(
            right,
            [block_of(0, block) for block in blocks],
            masks,
            row_ref,
            [lane_ref[block : block + 1, :] for block in blocks],
            lax.axis_index("half") * (parts // 2) + own_number(),
            size,
            put,
        )


def gather_lanes(x_ref, u_ref):
    size = x_ref.shape[0]
    cols = u_ref.shape[1]
    outer = u_ref.shape[0] // size
    for o in range(outer):
        for b in range(0, cols, PACK):
            at = o * cols + b
            got = pick_lanes(
                [x_ref[-d % size, at : at + PACK, :] for d in range(size)], 1, True
            )
            for v in range(size):
                u_ref[o * size + v, b : b + PACK, :] = turn_lanes(got[v], v, size)


def finish_rows(layer, at, step, u_ref, pair_ref, w_gate, w_out, gain_ref, bias_ref):
    _, cols_n, width = pair_ref.shape
    base = beside(pair_ref[at : at + step].reshape(step * cols_n, width))
    normed = norm_beside(base, gain_ref[layer, 0:1, :], bias_ref[layer, 0:1, :])
    gate = jax.nn.sigmoid(jnp.dot(normed, w_gate, preferred_element_type=jnp.float32))
    x = beside(u_ref[at : at + step].reshape(step * cols_n, width))
    y = norm_beside(x, gain_ref[layer, 1:2, :], bias_ref[layer, 1:2, :])
    update = jnp.dot(y, w_out, preferred_element_type=jnp.float32)
    return below((base.astype(jnp.float32) + gate * update).astype(jnp.bfloat16))


def middle_kernel(
    x_ref, pair_ref, w_gate_ref, w_out_ref, w_in_ref, gain_ref, bias_ref,
    mid_ref, send_ref, u_ref, l_ref, r_ref,
):
    rows_n, cols_n, width = pair_ref.shape
    size = send_ref.shape[0]
    gather_lanes(x_ref, u_ref)
    mid = finish_rows(
        0, 0, rows_n, u_ref, pair_ref, w_gate_ref[0], w_out_ref[0], gain_ref, bias_ref
    )
    mid_ref[...] = mid.reshape(rows_n, cols_n, width)
    normed = norm_rows(mid, gain_ref[1, 0:1, :], bias_ref[1, 0:1, :])
    left, right = gated(normed, w_in_ref[...], width)
    put_rolled(l_ref, 0, left, cols_n, size)
    put_rolled(r_ref, 0, right, cols_n, size)
    for side, ref in enumerate((l_ref, r_ref)):

        def put(d, at, part, ahead=side * rows_n):
            send_ref[d, ahead + at : ahead + at + PACK, :] = part

        scatter_lanes(ref, size, put)


def close_kernel(
    x_ref, pair_ref, w_gate_ref, w_out_ref, gain_ref, bias_ref, out_ref, u_ref
):
    rows_n, cols_n, width = pair_ref.shape
    gather_lanes(x_ref, u_ref)
    step = CLOSE_STEP
    for i in range(0, rows_n, step):
        out = finish_rows(
            1, i, step, u_ref, pair_ref, w_gate_ref[1], w_out_ref[1], gain_ref, bias_ref
        )
        out_ref[i : i + step] = out.reshape(step, cols_n, width)


VMEM = pl.BlockSpec(memory_space=pltpu.VMEM)
SMEM = pl.BlockSpec(memory_space=pltpu.SMEM)
HBM = pl.BlockSpec(memory_space=pltpu.HBM)


def call(body, name, specs, outs, scratch, flops, moved, grant=40 * 2**20):
    return pl.pallas_call(
        body,
        name=name,
        in_specs=specs,
        out_specs=jax.tree.map(lambda _: VMEM, outs),
        out_shape=outs,
        scratch_shapes=scratch,
        cost_estimate=pl.CostEstimate(flops=flops, bytes_accessed=moved, transcendentals=0),
        compiler_params=pltpu.CompilerParams(vmem_limit_bytes=grant),
    )


NEAR = ("sub", "col")
ALL = ("half", "sub", "col")


def fast(pair, residue_mask, norm_gain, norm_bias, w_in_q, exp_in, w_out_q, exp_out):
    rows_n, cols_n, width = pair.shape
    row_count, col_count = 2 * lax.axis_size("sub"), lax.axis_size("col")
    parts = row_count * col_count
    near = parts // 2
    own = width // parts
    tokens = residue_mask.shape[0]
    bf16, f32 = jnp.bfloat16, jnp.float32
    half = lax.axis_index("half")
    within = lax.axis_index("sub") * col_count + lax.axis_index("col")
    here = half * near + within
    mask = residue_mask.astype(f32)
    by_col = mask.reshape(tokens // cols_n, cols_n)
    lane_mask = jnp.tile(by_col, (1, own))
    half_mask = lax.dynamic_slice_in_dim(
        lane_mask, half * (lane_mask.shape[0] // 2), lane_mask.shape[0] // 2
    )
    row_mask = jnp.broadcast_to(mask[:, None], (tokens, width))
    def sum_mask(group):
        return jnp.repeat(jnp.roll(by_col, group, axis=1), own, axis=1)

    block = (rows_n, cols_n, width)
    sent = jax.ShapeDtypeStruct((parts, 2 * rows_n, width), bf16)
    back0 = jax.ShapeDtypeStruct((near, 2 * rows_n, width), bf16)
    back1 = jax.ShapeDtypeStruct((parts, rows_n, width), bf16)
    pairs = rows_n * cols_n
    proj_cost = (2 * pairs * width * 4 * width, 8 * pairs * width)
    product_cost = (2 * tokens * tokens * tokens * own * own, 6 * pairs * width)
    side = pltpu.VMEM(block, bf16)
    def exchange(x, axes=ALL):
        return lax.all_to_all(x, axes, 0, 0, tiled=True)

    turned = pltpu.VMEM((cols_n, rows_n, width), bf16)
    flat = pltpu.VMEM((pairs, width), f32)
    send, gain0 = call(
        right_kernel, "right0", [HBM] * 5,
        (sent, jax.ShapeDtypeStruct(norm_gain.shape, f32)),
        [
            side,
            pltpu.VMEM(norm_gain.shape, f32),
            pltpu.VMEM(norm_bias.shape, f32),
            pltpu.VMEM((1, width, 2 * width), bf16),
            pltpu.SMEM(exp_in.shape, jnp.int32),
            flat,
            turned,
            pltpu.SemaphoreType.DMA((5,)),
        ],
        *proj_cost, grant=None,
    )(pair, norm_gain, norm_bias, w_in_q, exp_in)
    right = exchange(send)

    chips = near // 2
    two = jax.ShapeDtypeStruct((2, 2 * rows_n, width), bf16)
    each = jax.ShapeDtypeStruct((chips, 2 * rows_n, width), bf16)
    mine, others = call(
        left_kernel, "left0", [VMEM, VMEM, VMEM, VMEM, SMEM], (each, each),
        [flat, turned, pltpu.VMEM((near, 2 * rows_n, width), bf16)], *proj_cost,
    )(pair, gain0, norm_bias, w_in_q, exp_in)

    def across(x, offset):
        return lax.ppermute(x, NEAR, [(n, n ^ offset) for n in range(near)])

    lefts = call(
        pack_kernel, "pack0", [VMEM, VMEM], (two,) * chips, [], 0, 4 * pairs * width
    )(mine, across(others, 1))
    lefts = [across(x, 2 * m) if m else x for x, m in zip(lefts, chip_order(chips))]

    doubled = jax.ShapeDtypeStruct((2, 2 * width, 2 * width), bf16)
    w_in, w_gate, w_out = call(
        functools.partial(weights_kernel, parts), "weights",
        [VMEM, VMEM, SMEM, VMEM, SMEM],
        (jax.ShapeDtypeStruct((width, 4 * width), bf16), doubled, doubled),
        [], 0, 16 * width * width,
    )(lefts[1], w_in_q, exp_in, w_out_q, exp_out)
    groups = (2 * within, 2 * within + 1, here)
    sum_masks = jnp.stack([sum_mask(group) for group in groups])
    x = call(
        functools.partial(product0_kernel, row_count, own), "product0",
        [VMEM] * (5 + chips), back0,
        [pltpu.VMEM((near, 2 * rows_n, width), bf16)], *product_cost,
    )(
        w_in, right, sum_masks, half_mask, row_mask, *lefts,
    )
    x = exchange(x, NEAR).reshape(back1.shape)
    mid, send = call(
        middle_kernel, "middle", [VMEM] * 7,
        (jax.ShapeDtypeStruct(block, bf16), sent), [side, side, side], *proj_cost,
    )(x, pair, w_gate, w_out, w_in, norm_gain, norm_bias)
    got = exchange(send)
    x = call(
        functools.partial(product1_kernel, row_count, own), "product1",
        [VMEM] * 4, back1, [], *product_cost,
    )(got, sum_masks, lane_mask, row_mask)
    x = exchange(x)
    return call(
        close_kernel, "close", [VMEM] * 6,
        jax.ShapeDtypeStruct(block, bf16), [side], *proj_cost,
    )(x, mid, w_gate, w_out, norm_gain, norm_bias)


def solution(mesh):
    row_count, col_count = mesh.shape["row"], mesh.shape["col"]
    parts = row_count * col_count

    def step(pair, *rest):
        width = pair.shape[2]
        rows_n, cols_n = pair.shape[0] // row_count, pair.shape[1] // col_count
        fits = (
            width == 128
            and width % parts == 0
            and parts & (parts - 1) == 0
            and row_count % 2 == 0
            and cols_n == parts
            and rows_n % cols_n == 0
            and cols_n % OPEN_STEP == 0
            and rows_n % CLOSE_STEP == 0
        )
        if fits:
            halves = jax.sharding.Mesh(
                mesh.devices.reshape(2, row_count // 2, col_count), ALL
            )
            body, over, placed = fast, halves, P(("half", "sub"), "col", None)
        else:
            body, over, placed = plain, mesh, P("row", "col", None)
        return jax.shard_map(
            body,
            mesh=over,
            in_specs=(placed,) + (P(),) * len(rest),
            out_specs=placed,
            check_vma=False,
        )(pair, *rest)

    return step
```

```python
import functools

import jax
import jax.numpy as jnp
from jax import lax
from jax.experimental import pallas as pl
from jax.experimental.pallas import tpu as pltpu
from jax.sharding import PartitionSpec as P

BLK = 32
AXES = ("row", "col")
EPS = 1e-05


def layer_norm(values, scale_vec, shift_vec):
    average = jnp.mean(values, axis=-1, keepdims=True)
    centred = values - average
    variance = jnp.mean(centred * centred, axis=-1, keepdims=True)
    return centred * lax.rsqrt(variance + EPS) * scale_vec + shift_vec


def dequantize(quantized, exponents, block_size):
    scales = jnp.exp2(exponents.astype(jnp.float32))
    scales = jnp.repeat(jnp.repeat(scales, block_size, axis=0), block_size, axis=1)
    return (quantized.astype(jnp.float32) * scales).astype(jnp.bfloat16)


def plain_update(layer, pair, row_mask, col_mask, norm_gain, norm_bias, w_in, w_out):
    rows_n, cols_n, width = pair.shape
    row_count, col_count = lax.axis_size("row"), lax.axis_size("col")
    parts = row_count * col_count
    own = width // parts
    normed = layer_norm(
        pair.astype(jnp.float32), norm_gain[layer, 0], norm_bias[layer, 0]
    ).astype(jnp.bfloat16)
    proj = jnp.einsum("ijc,cd->ijd", normed, w_in, preferred_element_type=jnp.float32)
    p0, p1, p2, p3, p4 = jnp.split(proj, 5, axis=-1)
    pm = (row_mask[:, None] * col_mask[None, :])[:, :, None]
    left = (jax.nn.sigmoid(p0) * p1 * pm).astype(jnp.bfloat16)
    right = (jax.nn.sigmoid(p2) * p3 * pm).astype(jnp.bfloat16)
    sent = jnp.stack([left, right]).reshape(2, rows_n, cols_n, parts, own)
    got = lax.all_to_all(sent.transpose(3, 0, 4, 1, 2), AXES, 0, 0, tiled=True)
    got = got.reshape(row_count, col_count, 2, own, rows_n, cols_n)
    whole = got.transpose(2, 3, 0, 4, 1, 5).reshape(
        2, own, row_count * rows_n, col_count * cols_n
    )
    spec = "cik,cjk->cij" if layer == 0 else "cki,ckj->cij"
    x = jnp.einsum(spec, whole[0], whole[1], preferred_element_type=jnp.float32)
    x = x.astype(jnp.bfloat16).reshape(own, row_count, rows_n, col_count, cols_n)
    back = x.transpose(1, 3, 0, 2, 4).reshape(parts, own, rows_n, cols_n)
    back = lax.all_to_all(back, AXES, 0, 0, tiled=True)
    x = back.transpose(2, 3, 0, 1).reshape(rows_n, cols_n, width)
    y = layer_norm(
        x.astype(jnp.float32), norm_gain[layer, 1], norm_bias[layer, 1]
    ).astype(jnp.bfloat16)
    out = jnp.einsum("ijc,cd->ijd", y, w_out, preferred_element_type=jnp.float32)
    return (pair.astype(jnp.float32) + jax.nn.sigmoid(p4) * out).astype(jnp.bfloat16)


def plain(pair, residue_mask, norm_gain, norm_bias, w_in_q, exp_in, w_out_q, exp_out):
    rows_n, cols_n, _ = pair.shape
    mask = residue_mask.astype(jnp.float32)
    row_mask = lax.dynamic_slice_in_dim(mask, lax.axis_index("row") * rows_n, rows_n)
    col_mask = lax.dynamic_slice_in_dim(mask, lax.axis_index("col") * cols_n, cols_n)
    for layer in range(2):
        w_in = dequantize(w_in_q[layer], exp_in[layer], BLK)
        w_out = dequantize(w_out_q[layer], exp_out[layer], BLK)
        pair = plain_update(
            layer, pair, row_mask, col_mask, norm_gain, norm_bias, w_in, w_out
        )
    return pair


PACK = 16


def pick_lanes(values, slot, back=False):
    size = len(values)
    lane = lax.broadcasted_iota(jnp.int32, values[0].shape, 1).astype(jnp.int16)
    step = 1
    while step < size:
        stay = (lane & jnp.int16(slot * step)) == 0
        move = -step if back else step
        values = [
            jnp.where(stay, values[v], values[(v + move) % size]) for v in range(size)
        ]
        step *= 2
    return values


def turn_lanes(value, by, size):
    if by == 0:
        return value
    lanes = value.shape[1]
    lane = lax.broadcasted_iota(jnp.int32, value.shape, 1).astype(jnp.int16)
    near = (lane & jnp.int16(size - 1)) < jnp.int16(size - by)
    return jnp.where(
        near, pltpu.roll(value, lanes - by, 1), pltpu.roll(value, size - by, 1)
    )


def twice(weights):
    none = jnp.zeros_like(weights)
    return jnp.concatenate(
        [
            jnp.concatenate([weights, none], axis=1),
            jnp.concatenate([none, weights], axis=1),
        ],
        axis=0,
    )


def beside(rows):
    half = rows.shape[0] // 2
    return jnp.concatenate([rows[:half], rows[half:]], axis=1)


def below(lanes):
    half = lanes.shape[1] // 2
    return jnp.concatenate([lanes[:, :half], lanes[:, half:]], axis=0)


def norm_beside(values, gain, bias):
    width = values.shape[1] // 2
    share = jnp.full((width, width), 1.0 / width, jnp.float32)
    row = lax.broadcasted_iota(jnp.int32, (width, width), 0)
    column = lax.broadcasted_iota(jnp.int32, (width, width), 1)
    centre = (row == column).astype(jnp.float32) - share
    centred = jnp.dot(
        values, twice(centre.astype(jnp.bfloat16)), preferred_element_type=jnp.float32
    )
    variance = jnp.dot(
        (centred * centred).astype(jnp.bfloat16),
        twice(share.astype(jnp.bfloat16)),
        preferred_element_type=jnp.float32,
    )
    gain = jnp.concatenate([gain, gain], axis=1)
    bias = jnp.concatenate([bias, bias], axis=1)
    return (centred * lax.rsqrt(variance + EPS) * gain + bias).astype(jnp.bfloat16)


def norm_rows(values, gain, bias):
    return below(norm_beside(beside(values), gain, bias))


def scaled(q_ref, exp_ref, layer, first, count, ahead=0):
    width = q_ref.shape[1]
    q = q_ref[layer, :, first * 128 : (first + count) * 128].astype(jnp.float32)
    scale = jnp.exp2(exp_ref[layer].astype(jnp.float32)).astype(jnp.bfloat16)
    blocks = scale.shape[1]
    row = lax.broadcasted_iota(jnp.int32, (blocks, count * 128), 0)
    column = lax.broadcasted_iota(jnp.int32, (blocks, count * 128), 1)
    spread = (row == (ahead + first) * (128 // BLK) + column // BLK).astype(jnp.bfloat16)
    scale = jnp.dot(scale, spread, preferred_element_type=jnp.float32)
    rows = [
        (q[rb * BLK : (rb + 1) * BLK] * scale[rb : rb + 1]).astype(jnp.bfloat16)
        for rb in range(width // BLK)
    ]
    return jnp.concatenate(rows, axis=0)


def slotted(weights, width, size):
    slot = width // size
    row = lax.broadcasted_iota(jnp.int32, (width, width), 0)
    column = lax.broadcasted_iota(jnp.int32, (width, width), 1)
    order = (row == column % slot * size + column // slot).astype(jnp.bfloat16)
    tiles = [
        jnp.dot(
            weights[:, t : t + width], order, preferred_element_type=jnp.float32
        ).astype(jnp.bfloat16)
        for t in range(0, weights.shape[1], width)
    ]
    return jnp.concatenate(tiles, axis=1)


def gated(normed, weights, width):
    proj = jnp.dot(normed, weights, preferred_element_type=jnp.float32)
    return [
        jax.nn.sigmoid(proj[:, t : t + width]) * proj[:, t + width : t + 2 * width]
        for t in range(0, proj.shape[1], 2 * width)
    ]


def put_rolled(ref, at, values, rows, size):
    slot = values.shape[1] // size
    for s in range(values.shape[0] // rows):
        part = values[s * rows : (s + 1) * rows]
        shift = (at + s) % size * slot
        if shift:
            part = pltpu.roll(part, shift, 1)
        ref[at + s] = part.astype(jnp.bfloat16)


def scatter_lanes(ref, size, put):
    rows = ref.shape[1]
    for o in range(ref.shape[0] // size):
        for b in range(0, rows, PACK):
            got = pick_lanes(
                [ref[o * size + v, b : b + PACK, :] for v in range(size)],
                ref.shape[2] // size,
            )
            for d in range(size):
                put(d, o * rows + b, got[-d % size])


OPEN_STEP = 16


def in_turn(count, first, second):
    ready = first(0)
    for n in range(count):
        following = first(n + 1) if n + 1 < count else None
        second(n, ready)
        ready = following


def own_number():
    return lax.axis_index("sub") * lax.axis_size("col") + lax.axis_index("col")


def operand(size, pair_ref, gain_ref, bias_ref, weights, t_ref, v_ref):
    rows_n, cols_n, width = pair_ref.shape
    gain, bias = gain_ref[0, 0:1, :], bias_ref[0, 0:1, :]
    t_ref[...] = pair_ref[...].astype(jnp.float32).reshape(t_ref.shape)
    step = OPEN_STEP

    def norm(n):
        part = jnp.concatenate(
            [
                t_ref[pl.ds(n * step + s, rows_n, stride=cols_n), :]
                for s in range(step)
            ],
            axis=0,
        )
        return norm_rows(part.astype(jnp.bfloat16), gain, bias)

    def project(n, normed):
        (made,) = gated(normed, weights, width)
        put_rolled(v_ref, n * step, made, rows_n, size)

    in_turn(cols_n // step, norm, project)


def right_kernel(
    pair_hbm, gain_hbm, bias_hbm, q_hbm, exp_hbm, send_ref, gain0_ref,
    pair_ref, gain_ref, bias_ref, q_ref, exp_ref, t_ref, v_ref, sems,
):
    first = q_ref.shape[2]
    moves = [
        pltpu.make_async_copy(source, target, sems.at[n])
        for n, (source, target) in enumerate(
            (
                (exp_hbm, exp_ref),
                (q_hbm.at[0:1, :, first : 2 * first], q_ref),
                (gain_hbm, gain_ref),
                (bias_hbm, bias_ref),
                (pair_hbm, pair_ref),
            )
        )
    ]
    for move in moves:
        move.start()
    for move in moves[:-1]:
        move.wait()
    width = pair_ref.shape[2]
    size = send_ref.shape[0]
    near = size // 2
    weights = slotted(scaled(q_ref, exp_ref, 0, 0, 2, 2), width, size)
    moves[-1].wait()
    gain0_ref[...] = gain_ref[...]
    operand(size, pair_ref, gain_ref, bias_ref, weights, t_ref, v_ref)
    rows = v_ref.shape[1]

    def put(d, at, part):
        at = d % 2 * rows + at
        send_ref[d // 2, at : at + PACK, :] = part
        send_ref[near + d // 2, at : at + PACK, :] = part

    scatter_lanes(v_ref, size, put)


def chip_order(chips):
    return [0, *range(chips // 2, chips), *range(1, chips // 2)]


def left_kernel(pair_ref, gain_ref, bias_ref, q_ref, exp_ref, *refs):
    own_ref, other_ref, t_ref, v_ref, o_ref = refs
    width = pair_ref.shape[2]
    size = 2 * o_ref.shape[0]
    weights = slotted(scaled(q_ref, exp_ref, 0, 0, 2), width, size)
    operand(size, pair_ref, gain_ref, bias_ref, weights, t_ref, v_ref)
    rows = v_ref.shape[1]
    here = own_number()

    def put(d, at, part):
        at = d % 2 * rows + at
        o_ref[here ^ (d // 2), at : at + PACK, :] = part

    scatter_lanes(v_ref, size, put)
    for n, m in enumerate(chip_order(own_ref.shape[0])):
        own_ref[n] = o_ref[2 * m]
        other_ref[n] = o_ref[2 * m + 1]


def pack_kernel(own_ref, other_ref, *outs):
    for n, out in enumerate(outs):
        out[0] = own_ref[n]
        out[1] = other_ref[n]


def weights_kernel(size, _, q_ref, exp_ref, o_ref, oexp_ref, in_ref, gate_ref, out_ref):
    width = q_ref.shape[1]
    in_ref[...] = slotted(scaled(q_ref, exp_ref, 1, 0, 4), width, size)
    for layer in range(2):
        gate_ref[layer] = twice(scaled(q_ref, exp_ref, layer, 4, 1))
        out_ref[layer] = twice(scaled(o_ref, oexp_ref, layer, 0, 1))


def channel_masks(sum_ref, own, lanes):
    channel = lax.broadcasted_iota(jnp.int32, (1, lanes), 1) % own
    return [
        [
            jnp.where(channel == a, sum_ref[t : t + 1, :], 0.0).astype(jnp.bfloat16)
            for t in range(sum_ref.shape[0])
        ]
        for a in range(own)
    ]


def multiply(right, blocks, masks, row_ref, lane_rows, group, size, put):
    lanes = blocks[0][0].shape[1]
    lane = lax.broadcasted_iota(jnp.int32, (1, lanes), 1)
    turn = (lane & -size) + ((lane - group) & (size - 1))
    turn = jnp.broadcast_to(turn, (right.shape[0], lanes))
    left = jnp.concatenate(
        [
            jnp.concatenate([part * mask for part, mask in zip(parts, row)], axis=1)
            for parts in blocks
            for row in masks
        ],
        axis=0,
    )
    x = lax.dot_general(
        right, left, (((1,), (1,)), ((), ())), preferred_element_type=jnp.float32
    )
    for h in range(len(blocks)):
        piece = x[:, h * lanes : (h + 1) * lanes] * row_ref[...] * lane_rows[h]
        piece = jnp.take_along_axis(piece, turn, axis=1, mode="promise_in_bounds")
        put(h, piece.astype(jnp.bfloat16))


def product0_kernel(
    row_count, own, _, right_ref, sum_ref, lane_ref, row_ref, *refs
):
    *left_refs, x_ref, l_ref = refs
    here = own_number()
    for ref, m in zip(left_refs, chip_order(len(left_refs))):
        l_ref[here ^ (2 * m)] = ref[0]
        l_ref[here ^ (2 * m + 1)] = ref[1]
    parts, both, lanes = right_ref.shape
    rows = both // 2
    col_count = parts // row_count
    size = lanes // own
    outer = rows // size
    tiles = sum_ref.shape[1]
    for t in range(2):
        masks = channel_masks(sum_ref.at[t], own, lanes)

        def block_of(ref, block):
            r, h = block // outer, block % outer
            at = t * rows + h * size
            return [
                ref[r * col_count + c, at : at + size, :] for c in range(tiles)
            ]

        right = jnp.concatenate(
            [
                jnp.concatenate(block_of(right_ref, block), axis=1)
                for block in range(tiles)
            ],
            axis=0,
        )
        for r in range(row_count // 2):

            def put(h, piece):
                at = t * rows + h * size
                for c in range(col_count):
                    x_ref[r * col_count + c, at : at + size, :] = piece[
                        c * size : (c + 1) * size, :
                    ]

            blocks = range(r * outer, (r + 1) * outer)
            multiply(
                right,
                [block_of(l_ref, block) for block in blocks],
                masks,
                row_ref,
                [lane_ref[block : block + 1, :] for block in blocks],
                2 * here + t,
                size,
                put,
            )


def product1_kernel(
    row_count, own, got_ref, sum_ref, lane_ref, row_ref, x_ref
):
    parts, both, lanes = got_ref.shape
    rows = both // 2
    col_count = parts // row_count
    size = lanes // own
    outer = rows // size
    tiles = lane_ref.shape[0]
    masks = channel_masks(sum_ref.at[2], own, lanes)

    def block_of(side, block):
        return [
            got_ref[
                t // outer * col_count + block,
                side * rows + t % outer * size : side * rows + (t % outer + 1) * size,
                :,
            ]
            for t in range(tiles)
        ]

    right = jnp.concatenate(
        [jnp.concatenate(block_of(1, block), axis=1) for block in range(tiles)], axis=0
    )
    for r in range(row_count):

        def put(h, piece):
            for c in range(col_count):
                x_ref[r * col_count + c, h * size : (h + 1) * size, :] = piece[
                    c * size : (c + 1) * size, :
                ]

        blocks = range(r * outer, (r + 1) * outer)
        multiply(
            right,
            [block_of(0, block) for block in blocks],
            masks,
            row_ref,
            [lane_ref[block : block + 1, :] for block in blocks],
            lax.axis_index("half") * (parts // 2) + own_number(),
            size,
            put,
        )


def gather_lanes(x_ref, u_ref):
    size = x_ref.shape[0]
    cols = u_ref.shape[1]
    outer = u_ref.shape[0] // size
    for o in range(outer):
        for b in range(0, cols, PACK):
            at = o * cols + b
            got = pick_lanes(
                [x_ref[-d % size, at : at + PACK, :] for d in range(size)], 1, True
            )
            for v in range(size):
                u_ref[o * size + v, b : b + PACK, :] = turn_lanes(got[v], v, size)


def finish_rows(layer, at, step, u_ref, pair_ref, w_gate, w_out, gain_ref, bias_ref):
    _, cols_n, width = pair_ref.shape
    base = beside(pair_ref[at : at + step].reshape(step * cols_n, width))
    normed = norm_beside(base, gain_ref[layer, 0:1, :], bias_ref[layer, 0:1, :])
    gate = jax.nn.sigmoid(jnp.dot(normed, w_gate, preferred_element_type=jnp.float32))
    x = beside(u_ref[at : at + step].reshape(step * cols_n, width))
    y = norm_beside(x, gain_ref[layer, 1:2, :], bias_ref[layer, 1:2, :])
    update = jnp.dot(y, w_out, preferred_element_type=jnp.float32)
    return below((base.astype(jnp.float32) + gate * update).astype(jnp.bfloat16))


def middle_kernel(
    x_ref, pair_ref, w_gate_ref, w_out_ref, w_in_ref, gain_ref, bias_ref,
    mid_ref, send_ref, u_ref, l_ref, r_ref,
):
    rows_n, cols_n, width = pair_ref.shape
    size = send_ref.shape[0]
    gather_lanes(x_ref, u_ref)
    mid = finish_rows(
        0, 0, rows_n, u_ref, pair_ref, w_gate_ref[0], w_out_ref[0], gain_ref, bias_ref
    )
    mid_ref[...] = mid.reshape(rows_n, cols_n, width)
    normed = norm_rows(mid, gain_ref[1, 0:1, :], bias_ref[1, 0:1, :])
    left, right = gated(normed, w_in_ref[...], width)
    put_rolled(l_ref, 0, left, cols_n, size)
    put_rolled(r_ref, 0, right, cols_n, size)
    for side, ref in enumerate((l_ref, r_ref)):

        def put(d, at, part, ahead=side * rows_n):
            send_ref[d, ahead + at : ahead + at + PACK, :] = part

        scatter_lanes(ref, size, put)


def close_kernel(
    x_ref, pair_ref, w_gate_ref, w_out_ref, gain_ref, bias_ref, out_ref, u_ref
):
    rows_n, cols_n, width = pair_ref.shape
    gather_lanes(x_ref, u_ref)
    out = finish_rows(
        1, 0, rows_n, u_ref, pair_ref, w_gate_ref[1], w_out_ref[1], gain_ref, bias_ref
    )
    out_ref[...] = out.reshape(rows_n, cols_n, width)


VMEM = pl.BlockSpec(memory_space=pltpu.VMEM)
HBM = pl.BlockSpec(memory_space=pltpu.HBM)


def call(body, name, specs, outs, scratch, flops, moved, grant=40 * 2**20):
    return pl.pallas_call(
        body,
        name=name,
        in_specs=specs,
        out_specs=jax.tree.map(lambda _: VMEM, outs),
        out_shape=outs,
        scratch_shapes=scratch,
        cost_estimate=pl.CostEstimate(flops=flops, bytes_accessed=moved, transcendentals=0),
        compiler_params=pltpu.CompilerParams(vmem_limit_bytes=grant),
    )


NEAR = ("sub", "col")
ALL = ("half", "sub", "col")


def fast(pair, residue_mask, norm_gain, norm_bias, w_in_q, exp_in, w_out_q, exp_out):
    rows_n, cols_n, width = pair.shape
    row_count, col_count = 2 * lax.axis_size("sub"), lax.axis_size("col")
    parts = row_count * col_count
    near = parts // 2
    own = width // parts
    tokens = residue_mask.shape[0]
    bf16, f32 = jnp.bfloat16, jnp.float32
    half = lax.axis_index("half")
    within = lax.axis_index("sub") * col_count + lax.axis_index("col")
    here = half * near + within
    mask = residue_mask.astype(f32)
    by_col = mask.reshape(tokens // cols_n, cols_n)
    lane_mask = jnp.tile(by_col, (1, own))
    half_mask = lax.dynamic_slice_in_dim(
        lane_mask, half * (lane_mask.shape[0] // 2), lane_mask.shape[0] // 2
    )
    row_mask = jnp.broadcast_to(mask[:, None], (tokens, width))
    def sum_mask(group):
        return jnp.repeat(jnp.roll(by_col, group, axis=1), own, axis=1)

    block = (rows_n, cols_n, width)
    sent = jax.ShapeDtypeStruct((parts, 2 * rows_n, width), bf16)
    back0 = jax.ShapeDtypeStruct((near, 2 * rows_n, width), bf16)
    back1 = jax.ShapeDtypeStruct((parts, rows_n, width), bf16)
    pairs = rows_n * cols_n
    proj_cost = (2 * pairs * width * 4 * width, 8 * pairs * width)
    product_cost = (2 * tokens * tokens * tokens * own * own, 6 * pairs * width)
    side = pltpu.VMEM(block, bf16)
    def exchange(x, axes=ALL):
        return lax.all_to_all(x, axes, 0, 0, tiled=True)

    turned = pltpu.VMEM((cols_n, rows_n, width), bf16)
    flat = pltpu.VMEM((pairs, width), f32)
    send, gain0 = call(
        right_kernel, "right0", [HBM] * 5,
        (sent, jax.ShapeDtypeStruct(norm_gain.shape, f32)),
        [
            side,
            pltpu.VMEM(norm_gain.shape, f32),
            pltpu.VMEM(norm_bias.shape, f32),
            pltpu.VMEM((1, width, 2 * width), bf16),
            pltpu.VMEM(exp_in.shape, jnp.int32),
            flat,
            turned,
            pltpu.SemaphoreType.DMA((5,)),
        ],
        *proj_cost, grant=None,
    )(pair, norm_gain, norm_bias, w_in_q, exp_in)
    right = exchange(send)

    chips = near // 2
    two = jax.ShapeDtypeStruct((2, 2 * rows_n, width), bf16)
    each = jax.ShapeDtypeStruct((chips, 2 * rows_n, width), bf16)
    mine, others = call(
        left_kernel, "left0", [VMEM] * 5, (each, each),
        [flat, turned, pltpu.VMEM((near, 2 * rows_n, width), bf16)], *proj_cost,
    )(pair, gain0, norm_bias, w_in_q, exp_in)

    def across(x, offset):
        return lax.ppermute(x, NEAR, [(n, n ^ offset) for n in range(near)])

    lefts = call(
        pack_kernel, "pack0", [VMEM, VMEM], (two,) * chips, [], 0, 4 * pairs * width
    )(mine, across(others, 1))
    lefts = [across(x, 2 * m) if m else x for x, m in zip(lefts, chip_order(chips))]

    doubled = jax.ShapeDtypeStruct((2, 2 * width, 2 * width), bf16)
    w_in, w_gate, w_out = call(
        functools.partial(weights_kernel, parts), "weights",
        [VMEM] * 5,
        (jax.ShapeDtypeStruct((width, 4 * width), bf16), doubled, doubled),
        [], 0, 16 * width * width,
    )(lefts[1], w_in_q, exp_in, w_out_q, exp_out)
    groups = (2 * within, 2 * within + 1, here)
    sum_masks = jnp.stack([sum_mask(group) for group in groups])
    x = call(
        functools.partial(product0_kernel, row_count, own), "product0",
        [VMEM] * (5 + chips), back0,
        [pltpu.VMEM((near, 2 * rows_n, width), bf16)], *product_cost,
    )(
        w_in, right, sum_masks, half_mask, row_mask, *lefts,
    )
    x = exchange(x, NEAR).reshape(back1.shape)
    mid, send = call(
        middle_kernel, "middle", [VMEM] * 7,
        (jax.ShapeDtypeStruct(block, bf16), sent), [side, side, side], *proj_cost,
    )(x, pair, w_gate, w_out, w_in, gain0, norm_bias)
    got = exchange(send)
    x = call(
        functools.partial(product1_kernel, row_count, own), "product1",
        [VMEM] * 4, back1, [], *product_cost,
    )(got, sum_masks, lane_mask, row_mask)
    x = exchange(x)
    return call(
        close_kernel, "close", [VMEM] * 6,
        jax.ShapeDtypeStruct(block, bf16), [side], *proj_cost,
    )(x, mid, w_gate, w_out, gain0, norm_bias)


def solution(mesh):
    row_count, col_count = mesh.shape["row"], mesh.shape["col"]
    parts = row_count * col_count

    def step(pair, *rest):
        width = pair.shape[2]
        rows_n, cols_n = pair.shape[0] // row_count, pair.shape[1] // col_count
        fits = (
            width == 128
            and width % parts == 0
            and parts & (parts - 1) == 0
            and row_count % 2 == 0
            and cols_n == parts
            and rows_n % cols_n == 0
            and cols_n % OPEN_STEP == 0
        )
        if fits:
            halves = jax.sharding.Mesh(
                mesh.devices.reshape(2, row_count // 2, col_count), ALL
            )
            body, over, placed = fast, halves, P(("half", "sub"), "col", None)
        else:
            body, over, placed = plain, mesh, P("row", "col", None)
        return jax.shard_map(
            body,
            mesh=over,
            in_specs=(placed,) + (P(),) * len(rest),
            out_specs=placed,
            check_vma=False,
        )(pair, *rest)

    return step
```

```python
import functools

import jax
import jax.numpy as jnp
from jax import lax
from jax.experimental import pallas as pl
from jax.experimental.pallas import tpu as pltpu
from jax.sharding import PartitionSpec as P

BLK = 32
AXES = ("row", "col")
EPS = 1e-05


def layer_norm(values, scale_vec, shift_vec):
    average = jnp.mean(values, axis=-1, keepdims=True)
    centred = values - average
    variance = jnp.mean(centred * centred, axis=-1, keepdims=True)
    return centred * lax.rsqrt(variance + EPS) * scale_vec + shift_vec


def dequantize(quantized, exponents, block_size):
    scales = jnp.exp2(exponents.astype(jnp.float32))
    scales = jnp.repeat(jnp.repeat(scales, block_size, axis=0), block_size, axis=1)
    return (quantized.astype(jnp.float32) * scales).astype(jnp.bfloat16)


def plain_update(layer, pair, row_mask, col_mask, norm_gain, norm_bias, w_in, w_out):
    rows_n, cols_n, width = pair.shape
    row_count, col_count = lax.axis_size("row"), lax.axis_size("col")
    parts = row_count * col_count
    own = width // parts
    normed = layer_norm(
        pair.astype(jnp.float32), norm_gain[layer, 0], norm_bias[layer, 0]
    ).astype(jnp.bfloat16)
    proj = jnp.einsum("ijc,cd->ijd", normed, w_in, preferred_element_type=jnp.float32)
    p0, p1, p2, p3, p4 = jnp.split(proj, 5, axis=-1)
    pm = (row_mask[:, None] * col_mask[None, :])[:, :, None]
    left = (jax.nn.sigmoid(p0) * p1 * pm).astype(jnp.bfloat16)
    right = (jax.nn.sigmoid(p2) * p3 * pm).astype(jnp.bfloat16)
    sent = jnp.stack([left, right]).reshape(2, rows_n, cols_n, parts, own)
    got = lax.all_to_all(sent.transpose(3, 0, 4, 1, 2), AXES, 0, 0, tiled=True)
    got = got.reshape(row_count, col_count, 2, own, rows_n, cols_n)
    whole = got.transpose(2, 3, 0, 4, 1, 5).reshape(
        2, own, row_count * rows_n, col_count * cols_n
    )
    spec = "cik,cjk->cij" if layer == 0 else "cki,ckj->cij"
    x = jnp.einsum(spec, whole[0], whole[1], preferred_element_type=jnp.float32)
    x = x.astype(jnp.bfloat16).reshape(own, row_count, rows_n, col_count, cols_n)
    back = x.transpose(1, 3, 0, 2, 4).reshape(parts, own, rows_n, cols_n)
    back = lax.all_to_all(back, AXES, 0, 0, tiled=True)
    x = back.transpose(2, 3, 0, 1).reshape(rows_n, cols_n, width)
    y = layer_norm(
        x.astype(jnp.float32), norm_gain[layer, 1], norm_bias[layer, 1]
    ).astype(jnp.bfloat16)
    out = jnp.einsum("ijc,cd->ijd", y, w_out, preferred_element_type=jnp.float32)
    return (pair.astype(jnp.float32) + jax.nn.sigmoid(p4) * out).astype(jnp.bfloat16)


def plain(pair, residue_mask, norm_gain, norm_bias, w_in_q, exp_in, w_out_q, exp_out):
    rows_n, cols_n, _ = pair.shape
    mask = residue_mask.astype(jnp.float32)
    row_mask = lax.dynamic_slice_in_dim(mask, lax.axis_index("row") * rows_n, rows_n)
    col_mask = lax.dynamic_slice_in_dim(mask, lax.axis_index("col") * cols_n, cols_n)
    for layer in range(2):
        w_in = dequantize(w_in_q[layer], exp_in[layer], BLK)
        w_out = dequantize(w_out_q[layer], exp_out[layer], BLK)
        pair = plain_update(
            layer, pair, row_mask, col_mask, norm_gain, norm_bias, w_in, w_out
        )
    return pair


PACK = 16


def pick_lanes(values, slot, back=False):
    size = len(values)
    lane = lax.broadcasted_iota(jnp.int32, values[0].shape, 1).astype(jnp.int16)
    step = 1
    while step < size:
        stay = (lane & jnp.int16(slot * step)) == 0
        move = -step if back else step
        values = [
            jnp.where(stay, values[v], values[(v + move) % size]) for v in range(size)
        ]
        step *= 2
    return values


def turn_lanes(value, by, size):
    if by == 0:
        return value
    lanes = value.shape[1]
    lane = lax.broadcasted_iota(jnp.int32, value.shape, 1).astype(jnp.int16)
    near = (lane & jnp.int16(size - 1)) < jnp.int16(size - by)
    return jnp.where(
        near, pltpu.roll(value, lanes - by, 1), pltpu.roll(value, size - by, 1)
    )


def twice(weights):
    none = jnp.zeros_like(weights)
    return jnp.concatenate(
        [
            jnp.concatenate([weights, none], axis=1),
            jnp.concatenate([none, weights], axis=1),
        ],
        axis=0,
    )


def beside(rows):
    half = rows.shape[0] // 2
    return jnp.concatenate([rows[:half], rows[half:]], axis=1)


def below(lanes):
    half = lanes.shape[1] // 2
    return jnp.concatenate([lanes[:, :half], lanes[:, half:]], axis=0)


def norm_beside(values, gain, bias):
    width = values.shape[1] // 2
    share = jnp.full((width, width), 1.0 / width, jnp.float32)
    row = lax.broadcasted_iota(jnp.int32, (width, width), 0)
    column = lax.broadcasted_iota(jnp.int32, (width, width), 1)
    centre = (row == column).astype(jnp.float32) - share
    centred = jnp.dot(
        values, twice(centre.astype(jnp.bfloat16)), preferred_element_type=jnp.float32
    )
    variance = jnp.dot(
        (centred * centred).astype(jnp.bfloat16),
        twice(share.astype(jnp.bfloat16)),
        preferred_element_type=jnp.float32,
    )
    gain = jnp.concatenate([gain, gain], axis=1)
    bias = jnp.concatenate([bias, bias], axis=1)
    return (centred * lax.rsqrt(variance + EPS) * gain + bias).astype(jnp.bfloat16)


def norm_rows(values, gain, bias):
    return below(norm_beside(beside(values), gain, bias))


def scaled(q_ref, exp_ref, layer, first, count, ahead=0):
    width = q_ref.shape[1]
    q = q_ref[layer, :, first * 128 : (first + count) * 128].astype(jnp.float32)
    scale = jnp.exp2(exp_ref[layer].astype(jnp.float32)).astype(jnp.bfloat16)
    blocks = scale.shape[1]
    row = lax.broadcasted_iota(jnp.int32, (blocks, count * 128), 0)
    column = lax.broadcasted_iota(jnp.int32, (blocks, count * 128), 1)
    spread = (row == (ahead + first) * (128 // BLK) + column // BLK).astype(jnp.bfloat16)
    scale = jnp.dot(scale, spread, preferred_element_type=jnp.float32)
    rows = [
        (q[rb * BLK : (rb + 1) * BLK] * scale[rb : rb + 1]).astype(jnp.bfloat16)
        for rb in range(width // BLK)
    ]
    return jnp.concatenate(rows, axis=0)


def slotted(weights, width, size):
    slot = width // size
    row = lax.broadcasted_iota(jnp.int32, (width, width), 0)
    column = lax.broadcasted_iota(jnp.int32, (width, width), 1)
    order = (row == column % slot * size + column // slot).astype(jnp.bfloat16)
    tiles = [
        jnp.dot(
            weights[:, t : t + width], order, preferred_element_type=jnp.float32
        ).astype(jnp.bfloat16)
        for t in range(0, weights.shape[1], width)
    ]
    return jnp.concatenate(tiles, axis=1)


def gated(normed, weights, width):
    proj = jnp.dot(normed, weights, preferred_element_type=jnp.float32)
    return [
        jax.nn.sigmoid(proj[:, t : t + width]) * proj[:, t + width : t + 2 * width]
        for t in range(0, proj.shape[1], 2 * width)
    ]


def put_rolled(ref, at, values, rows, size):
    slot = values.shape[1] // size
    for s in range(values.shape[0] // rows):
        part = values[s * rows : (s + 1) * rows]
        shift = (at + s) % size * slot
        if shift:
            part = pltpu.roll(part, shift, 1)
        ref[at + s] = part.astype(jnp.bfloat16)


def scatter_lanes(ref, size, put):
    rows = ref.shape[1]
    for o in range(ref.shape[0] // size):
        for b in range(0, rows, PACK):
            got = pick_lanes(
                [ref[o * size + v, b : b + PACK, :] for v in range(size)],
                ref.shape[2] // size,
            )
            for d in range(size):
                put(d, o * rows + b, got[-d % size])


OPEN_STEP = 16


def in_turn(count, first, second):
    ready = first(0)
    for n in range(count):
        following = first(n + 1) if n + 1 < count else None
        second(n, ready)
        ready = following


def own_number():
    return lax.axis_index("sub") * lax.axis_size("col") + lax.axis_index("col")


def operand(size, pair_ref, gain_ref, bias_ref, weights, t_ref, v_ref):
    rows_n, cols_n, width = pair_ref.shape
    gain, bias = gain_ref[0, 0:1, :], bias_ref[0, 0:1, :]
    t_ref[...] = pair_ref[...].astype(jnp.float32).reshape(t_ref.shape)
    step = OPEN_STEP

    def norm(n):
        part = jnp.concatenate(
            [
                t_ref[pl.ds(n * step + s, rows_n, stride=cols_n), :]
                for s in range(step)
            ],
            axis=0,
        )
        return norm_rows(part.astype(jnp.bfloat16), gain, bias)

    def project(n, normed):
        (made,) = gated(normed, weights, width)
        put_rolled(v_ref, n * step, made, rows_n, size)

    in_turn(cols_n // step, norm, project)


def right_kernel(
    pair_hbm, gain_hbm, bias_hbm, q_hbm, exp_hbm, send_ref, gain0_ref,
    pair_ref, gain_ref, bias_ref, q_ref, exp_ref, t_ref, v_ref, sems,
):
    first = q_ref.shape[2]
    moves = [
        pltpu.make_async_copy(source, target, sems.at[n])
        for n, (source, target) in enumerate(
            (
                (exp_hbm, exp_ref),
                (q_hbm.at[0:1, :, first : 2 * first], q_ref),
                (gain_hbm, gain_ref),
                (bias_hbm, bias_ref),
                (pair_hbm, pair_ref),
            )
        )
    ]
    for move in moves:
        move.start()
    for move in moves[:-1]:
        move.wait()
    width = pair_ref.shape[2]
    size = send_ref.shape[0]
    near = size // 2
    weights = slotted(scaled(q_ref, exp_ref, 0, 0, 2, 2), width, size)
    moves[-1].wait()
    gain0_ref[...] = gain_ref[...]
    operand(size, pair_ref, gain_ref, bias_ref, weights, t_ref, v_ref)
    rows = v_ref.shape[1]

    def put(d, at, part):
        at = d % 2 * rows + at
        send_ref[d // 2, at : at + PACK, :] = part
        send_ref[near + d // 2, at : at + PACK, :] = part

    scatter_lanes(v_ref, size, put)


def chip_order(chips):
    return [0, *range(chips // 2, chips), *range(1, chips // 2)]


def left_kernel(pair_ref, gain_ref, bias_ref, q_ref, exp_ref, *refs):
    own_ref, other_ref, t_ref, v_ref, o_ref = refs
    width = pair_ref.shape[2]
    size = 2 * o_ref.shape[0]
    weights = slotted(scaled(q_ref, exp_ref, 0, 0, 2), width, size)
    operand(size, pair_ref, gain_ref, bias_ref, weights, t_ref, v_ref)
    rows = v_ref.shape[1]
    here = own_number()

    def put(d, at, part):
        at = d % 2 * rows + at
        o_ref[here ^ (d // 2), at : at + PACK, :] = part

    scatter_lanes(v_ref, size, put)
    for n, m in enumerate(chip_order(own_ref.shape[0])):
        own_ref[n] = o_ref[2 * m]
        other_ref[n] = o_ref[2 * m + 1]


def pack_kernel(own_ref, other_ref, *outs):
    for n, out in enumerate(outs):
        out[0] = own_ref[n]
        out[1] = other_ref[n]


def weights_kernel(size, _, q_ref, exp_ref, o_ref, oexp_ref, in_ref, gate_ref, out_ref):
    width = q_ref.shape[1]
    in_ref[...] = slotted(scaled(q_ref, exp_ref, 1, 0, 4), width, size)
    for layer in range(2):
        gate_ref[layer] = twice(scaled(q_ref, exp_ref, layer, 4, 1))
        out_ref[layer] = twice(scaled(o_ref, oexp_ref, layer, 0, 1))


def channel_masks(sum_ref, own, lanes):
    channel = lax.broadcasted_iota(jnp.int32, (1, lanes), 1) % own
    return [
        [
            jnp.where(channel == a, sum_ref[t : t + 1, :], 0.0).astype(jnp.bfloat16)
            for t in range(sum_ref.shape[0])
        ]
        for a in range(own)
    ]


def multiply(right, blocks, masks, row_ref, lane_rows, group, size, put):
    lanes = blocks[0][0].shape[1]
    lane = lax.broadcasted_iota(jnp.int32, (1, lanes), 1)
    turn = (lane & -size) + ((lane - group) & (size - 1))
    turn = jnp.broadcast_to(turn, (right.shape[0], lanes))
    left = jnp.concatenate(
        [
            jnp.concatenate([part * mask for part, mask in zip(parts, row)], axis=1)
            for parts in blocks
            for row in masks
        ],
        axis=0,
    )
    x = lax.dot_general(
        right, left, (((1,), (1,)), ((), ())), preferred_element_type=jnp.float32
    )
    for h in range(len(blocks)):
        piece = x[:, h * lanes : (h + 1) * lanes] * row_ref[...] * lane_rows[h]
        piece = jnp.take_along_axis(piece, turn, axis=1, mode="promise_in_bounds")
        put(h, piece.astype(jnp.bfloat16))


def product0_kernel(
    row_count, own, _, right_ref, sum_ref, lane_ref, row_ref, *refs
):
    *left_refs, x_ref, l_ref = refs
    here = own_number()
    for ref, m in zip(left_refs, chip_order(len(left_refs))):
        l_ref[here ^ (2 * m)] = ref[0]
        l_ref[here ^ (2 * m + 1)] = ref[1]
    parts, both, lanes = right_ref.shape
    rows = both // 2
    col_count = parts // row_count
    size = lanes // own
    outer = rows // size
    tiles = sum_ref.shape[1]
    for t in range(2):
        masks = channel_masks(sum_ref.at[t], own, lanes)

        def block_of(ref, block):
            r, h = block // outer, block % outer
            at = t * rows + h * size
            return [
                ref[r * col_count + c, at : at + size, :] for c in range(tiles)
            ]

        right = jnp.concatenate(
            [
                jnp.concatenate(block_of(right_ref, block), axis=1)
                for block in range(tiles)
            ],
            axis=0,
        )
        for r in range(row_count // 2):

            def put(h, piece):
                at = t * rows + h * size
                for c in range(col_count):
                    x_ref[r * col_count + c, at : at + size, :] = piece[
                        c * size : (c + 1) * size, :
                    ]

            blocks = range(r * outer, (r + 1) * outer)
            multiply(
                right,
                [block_of(l_ref, block) for block in blocks],
                masks,
                row_ref,
                [lane_ref[block : block + 1, :] for block in blocks],
                2 * here + t,
                size,
                put,
            )


def product1_kernel(
    row_count, own, got_ref, sum_ref, lane_ref, row_ref, x_ref
):
    parts, both, lanes = got_ref.shape
    rows = both // 2
    col_count = parts // row_count
    size = lanes // own
    outer = rows // size
    tiles = lane_ref.shape[0]
    masks = channel_masks(sum_ref.at[2], own, lanes)

    def block_of(side, block):
        return [
            got_ref[
                t // outer * col_count + block,
                side * rows + t % outer * size : side * rows + (t % outer + 1) * size,
                :,
            ]
            for t in range(tiles)
        ]

    right = jnp.concatenate(
        [jnp.concatenate(block_of(1, block), axis=1) for block in range(tiles)], axis=0
    )
    for r in range(row_count):

        def put(h, piece):
            for c in range(col_count):
                x_ref[r * col_count + c, h * size : (h + 1) * size, :] = piece[
                    c * size : (c + 1) * size, :
                ]

        blocks = range(r * outer, (r + 1) * outer)
        multiply(
            right,
            [block_of(0, block) for block in blocks],
            masks,
            row_ref,
            [lane_ref[block : block + 1, :] for block in blocks],
            lax.axis_index("half") * (parts // 2) + own_number(),
            size,
            put,
        )


def gather_lanes(x_ref, u_ref):
    size = x_ref.shape[0]
    cols = u_ref.shape[1]
    outer = u_ref.shape[0] // size
    for o in range(outer):
        for b in range(0, cols, PACK):
            at = o * cols + b
            got = pick_lanes(
                [x_ref[-d % size, at : at + PACK, :] for d in range(size)], 1, True
            )
            for v in range(size):
                u_ref[o * size + v, b : b + PACK, :] = turn_lanes(got[v], v, size)


def gate_rows(layer, pair_ref, w_gate, gain_ref, bias_ref):
    rows_n, cols_n, width = pair_ref.shape
    base = beside(pair_ref[...].reshape(rows_n * cols_n, width))
    normed = norm_beside(base, gain_ref[layer, 0:1, :], bias_ref[layer, 0:1, :])
    gate = jax.nn.sigmoid(jnp.dot(normed, w_gate, preferred_element_type=jnp.float32))
    return base, gate


def finish_rows(layer, base, gate, u_ref, w_out, gain_ref, bias_ref):
    x = beside(u_ref[...].reshape(-1, u_ref.shape[2]))
    y = norm_beside(x, gain_ref[layer, 1:2, :], bias_ref[layer, 1:2, :])
    update = jnp.dot(y, w_out, preferred_element_type=jnp.float32)
    return below((base.astype(jnp.float32) + gate * update).astype(jnp.bfloat16))


def middle_kernel(
    x_ref, pair_ref, w_gate_ref, w_out_ref, w_in_ref, gain_ref, bias_ref,
    mid_ref, send_ref, u_ref, l_ref, r_ref,
):
    rows_n, cols_n, width = pair_ref.shape
    size = send_ref.shape[0]
    base, gate = gate_rows(0, pair_ref, w_gate_ref[0], gain_ref, bias_ref)
    gather_lanes(x_ref, u_ref)
    mid = finish_rows(0, base, gate, u_ref, w_out_ref[0], gain_ref, bias_ref)
    mid_ref[...] = mid.reshape(rows_n, cols_n, width)
    normed = norm_rows(mid, gain_ref[1, 0:1, :], bias_ref[1, 0:1, :])
    left, right = gated(normed, w_in_ref[...], width)
    put_rolled(l_ref, 0, left, cols_n, size)
    put_rolled(r_ref, 0, right, cols_n, size)
    for side, ref in enumerate((l_ref, r_ref)):

        def put(d, at, part, ahead=side * rows_n):
            send_ref[d, ahead + at : ahead + at + PACK, :] = part

        scatter_lanes(ref, size, put)


def close_kernel(
    x_ref, pair_ref, w_gate_ref, w_out_ref, gain_ref, bias_ref, out_ref, u_ref
):
    rows_n, cols_n, width = pair_ref.shape
    base, gate = gate_rows(1, pair_ref, w_gate_ref[1], gain_ref, bias_ref)
    gather_lanes(x_ref, u_ref)
    out = finish_rows(1, base, gate, u_ref, w_out_ref[1], gain_ref, bias_ref)
    out_ref[...] = out.reshape(rows_n, cols_n, width)


VMEM = pl.BlockSpec(memory_space=pltpu.VMEM)
HBM = pl.BlockSpec(memory_space=pltpu.HBM)


def call(body, name, specs, outs, scratch, flops, moved, grant=40 * 2**20):
    return pl.pallas_call(
        body,
        name=name,
        in_specs=specs,
        out_specs=jax.tree.map(lambda _: VMEM, outs),
        out_shape=outs,
        scratch_shapes=scratch,
        cost_estimate=pl.CostEstimate(flops=flops, bytes_accessed=moved, transcendentals=0),
        compiler_params=pltpu.CompilerParams(
            vmem_limit_bytes=grant
        ),
    )


NEAR = ("sub", "col")
ALL = ("half", "sub", "col")


def fast(pair, residue_mask, norm_gain, norm_bias, w_in_q, exp_in, w_out_q, exp_out):
    rows_n, cols_n, width = pair.shape
    row_count, col_count = 2 * lax.axis_size("sub"), lax.axis_size("col")
    parts = row_count * col_count
    near = parts // 2
    own = width // parts
    tokens = residue_mask.shape[0]
    bf16, f32 = jnp.bfloat16, jnp.float32
    half = lax.axis_index("half")
    within = lax.axis_index("sub") * col_count + lax.axis_index("col")
    here = half * near + within
    mask = residue_mask.astype(f32)
    by_col = mask.reshape(tokens // cols_n, cols_n)
    lane_mask = jnp.tile(by_col, (1, own))
    half_mask = lax.dynamic_slice_in_dim(
        lane_mask, half * (lane_mask.shape[0] // 2), lane_mask.shape[0] // 2
    )
    row_mask = jnp.broadcast_to(mask[:, None], (tokens, width))
    def sum_mask(group):
        return jnp.repeat(jnp.roll(by_col, group, axis=1), own, axis=1)

    block = (rows_n, cols_n, width)
    sent = jax.ShapeDtypeStruct((parts, 2 * rows_n, width), bf16)
    back0 = jax.ShapeDtypeStruct((near, 2 * rows_n, width), bf16)
    back1 = jax.ShapeDtypeStruct((parts, rows_n, width), bf16)
    pairs = rows_n * cols_n
    proj_cost = (2 * pairs * width * 4 * width, 8 * pairs * width)
    product_cost = (2 * tokens * tokens * tokens * own * own, 6 * pairs * width)
    side = pltpu.VMEM(block, bf16)
    def exchange(x, axes=ALL):
        return lax.all_to_all(x, axes, 0, 0, tiled=True)

    turned = pltpu.VMEM((cols_n, rows_n, width), bf16)
    flat = pltpu.VMEM((pairs, width), f32)
    send, gain0 = call(
        right_kernel, "right0", [HBM] * 5,
        (sent, jax.ShapeDtypeStruct(norm_gain.shape, f32)),
        [
            side,
            pltpu.VMEM(norm_gain.shape, f32),
            pltpu.VMEM(norm_bias.shape, f32),
            pltpu.VMEM((1, width, 2 * width), bf16),
            pltpu.VMEM(exp_in.shape, jnp.int32),
            flat,
            turned,
            pltpu.SemaphoreType.DMA((5,)),
        ],
        *proj_cost, grant=None,
    )(pair, norm_gain, norm_bias, w_in_q, exp_in)
    right = exchange(send)

    chips = near // 2
    two = jax.ShapeDtypeStruct((2, 2 * rows_n, width), bf16)
    each = jax.ShapeDtypeStruct((chips, 2 * rows_n, width), bf16)
    mine, others = call(
        left_kernel, "left0", [VMEM] * 5, (each, each),
        [flat, turned, pltpu.VMEM((near, 2 * rows_n, width), bf16)], *proj_cost,
    )(pair, gain0, norm_bias, w_in_q, exp_in)

    def across(x, offset):
        return lax.ppermute(x, NEAR, [(n, n ^ offset) for n in range(near)])

    lefts = call(
        pack_kernel, "pack0", [VMEM, VMEM], (two,) * chips, [], 0, 4 * pairs * width
    )(mine, across(others, 1))
    lefts = [across(x, 2 * m) if m else x for x, m in zip(lefts, chip_order(chips))]

    doubled = jax.ShapeDtypeStruct((2, 2 * width, 2 * width), bf16)
    w_in, w_gate, w_out = call(
        functools.partial(weights_kernel, parts), "weights",
        [VMEM] * 5,
        (jax.ShapeDtypeStruct((width, 4 * width), bf16), doubled, doubled),
        [], 0, 16 * width * width,
    )(lefts[1], w_in_q, exp_in, w_out_q, exp_out)
    groups = (2 * within, 2 * within + 1, here)
    sum_masks = jnp.stack([sum_mask(group) for group in groups])
    x = call(
        functools.partial(product0_kernel, row_count, own), "product0",
        [VMEM] * (5 + chips), back0,
        [pltpu.VMEM((near, 2 * rows_n, width), bf16)], *product_cost,
    )(
        w_in, right, sum_masks, half_mask, row_mask, *lefts,
    )
    x = exchange(x, NEAR).reshape(back1.shape)
    mid, send = call(
        middle_kernel, "middle", [VMEM] * 7,
        (jax.ShapeDtypeStruct(block, bf16), sent), [side, side, side], *proj_cost,
    )(x, pair, w_gate, w_out, w_in, gain0, norm_bias)
    got = exchange(send)
    x = call(
        functools.partial(product1_kernel, row_count, own), "product1",
        [VMEM] * 4, back1, [], *product_cost,
    )(got, sum_masks, lane_mask, row_mask)
    x = exchange(x)
    return call(
        close_kernel, "close", [VMEM] * 6,
        jax.ShapeDtypeStruct(block, bf16), [side], *proj_cost,
    )(x, mid, w_gate, w_out, gain0, norm_bias)


def solution(mesh):
    row_count, col_count = mesh.shape["row"], mesh.shape["col"]
    parts = row_count * col_count

    def step(pair, *rest):
        width = pair.shape[2]
        rows_n, cols_n = pair.shape[0] // row_count, pair.shape[1] // col_count
        fits = (
            width == 128
            and width % parts == 0
            and parts & (parts - 1) == 0
            and row_count % 2 == 0
            and cols_n == parts
            and rows_n % cols_n == 0
            and cols_n % OPEN_STEP == 0
        )
        if fits:
            halves = jax.sharding.Mesh(
                mesh.devices.reshape(2, row_count // 2, col_count), ALL
            )
            body, over, placed = fast, halves, P(("half", "sub"), "col", None)
        else:
            body, over, placed = plain, mesh, P("row", "col", None)
        return jax.shard_map(
            body,
            mesh=over,
            in_specs=(placed,) + (P(),) * len(rest),
            out_specs=placed,
            check_vma=False,
        )(pair, *rest)

    return step
```
